32 devices in a mesh: dp: 4 (over z), expert: 8 (over y, x, core).
Axes of the slice: x: 2, y: 2, z: 4, core: 2. Of those that a mesh axis runs over, the one named last changes fastest.
Arguments:
- grad_out: bfloat16 [4096, 2048], P(('dp', 'expert')), may hold values from -6 to 6
- saved_pre: bfloat16 [4096, 2, 768], P(('dp', 'expert')), may hold values from -6 to 6
- gate_probs: bfloat16 [4096, 2], P(('dp', 'expert')), may hold values from 0.019897461 to 0.19921875
- routes: int32 [4096, 2], P(('dp', 'expert')), may hold values from 0 to 15, all different within a row; in each aligned block of 128 rows (0 to 127, 128 to 255, ...) at most 32 rows name the same one
- down_weight: bfloat16 [16, 384, 2048], P('expert'), may hold values from -0.125 to 0.125
Outputs:
- grad_pre: bfloat16 [4096, 2, 768], P(('dp', 'expert'))
- grad_probs: bfloat16 [4096, 2], P(('dp', 'expert'))
- grad_down: bfloat16 [16, 384, 2048], P('expert', None, 'dp')
The draws below stay inside these ranges and needn't reach their ends.
Inputs may be any that keep to these rules, and one draw needn't show every extreme that they name: `routes`: the 2 experts of a token differ. Among the 128 tokens of one device no expert is named more than 32 times, and in every draw some expert is named exactly 32 times by the tokens of some device.
All inputs are finite; a program needn't handle non-finite values.
Results may differ from the reference program's by a relative error of at most 0.022.
Values may be sent and summed in bfloat16 or wider, within the bound.
No kernel may reach another device: no remote copies, remote signals or barrier semaphores. Data moves between devices by JAX's collectives and lax.ppermute only.
A program may use at most 64 MiB of HBM per device.

```python
import math
import jax
import jax.numpy as jnp
import numpy as np
from jax import lax

D = 2048
HID = 384
TOP = 2
TOK_DEV = 128
EXPERTS = 16
CAP = 32
TOKENS = 4096
N_DP = 4
N_EXPERT = 8


def strengthened(values, stream_key, source, target, blocks, factor):
    def block_of(dim):
        return (jnp.arange(values.shape[dim]) // (values.shape[dim] // blocks)).reshape((-1,) + (1,) * (values.ndim - 1 - dim))

    first = jax.random.permutation(stream_key, blocks)[block_of(target)]
    other_side = (block_of(target) + blocks // 2) % blocks
    return jnp.where((block_of(source) == first) | (block_of(source) == other_side), factor * values, values)


def level_of(key, shape, cuts, smallest, largest):
    level = 1.0
    for dim, shards_of in cuts:
        steps = jax.random.uniform(jax.random.fold_in(jax.random.fold_in(key, 6), dim), (shards_of,), jnp.float32, smallest / len(cuts), largest / len(cuts))
        level = level * jnp.repeat(jnp.exp(steps), shape[dim] // shards_of).reshape((-1,) + (1,) * (len(shape) - 1 - dim))
    return level


def shared_out(key, own, number, rows, count, top, limit, slope):
    sequence = jax.random.permutation(key, count)
    heavy_load, ordinary = portions_of(count, rows * top, limit, slope, True), portions_of(count, rows * top, limit, slope, False)
    places = jnp.arange(count)

    def named(lengths, offset_by):
        used = int((lengths > 0).sum())
        fixed = max(1, used // 4)
        passed = fixed + (places - fixed + offset_by * (used - fixed)) % max(1, count - fixed)
        return jnp.zeros((count,), jnp.int32).at[sequence[jnp.where(places < fixed, places, passed)]].set(jnp.asarray(lengths, jnp.int32))

    lengths = jnp.where(number % 4 == 0, named(heavy_load, number // 4), named(ordinary, number - number // 4 - 1))
    mixed = jax.random.permutation(jax.random.fold_in(own, 3), count)
    giver, taker = mixed[0:count // 2 * 2:2], mixed[1:count // 2 * 2:2]
    room = jnp.minimum(lengths[giver] - 1, limit - lengths[taker]) // 2
    room = jnp.where((giver == sequence[0]) | (taker == sequence[0]) | (lengths[taker] == 0), 0, jnp.maximum(room, 0))
    passed = jax.random.randint(jax.random.fold_in(own, 4), (count // 2,), 0, 1 << 20) % (room + 1)
    lengths = lengths.at[giver].add(-passed).at[taker].add(passed)
    items = jnp.searchsorted(jnp.cumsum(lengths), jnp.arange(rows * top), side="right").astype(jnp.int32)
    table = items.reshape(top, rows).T
    table = table[jax.random.permutation(jax.random.fold_in(own, 1), rows)]
    offset_by = jax.random.randint(jax.random.fold_in(own, 2), (rows, 1), 0, top)
    return jnp.take_along_axis(table, (jnp.arange(top)[None, :] + offset_by) % top, axis=1)


def portions_of(count, total, limit, slope, full):
    weights = [(1 << 20) // math.isqrt(grade ** slope) + 1 for grade in range(1, count + 1)]
    largest = limit if full else min(limit, max(-(-total // count), total * weights[0] // sum(weights)))
    least = 1 if total - largest >= count - 1 else 0
    given, spare = [largest] + [least] * (count - 1), total - largest - least * (count - 1)
    while spare > 0:
        movable = [i for i in range(1, count) if given[i] < largest] or [i for i in range(1, count) if given[i] < limit]
        mass, remaining = sum([weights[i] for i in movable]), spare
        for i in movable:
            addition = min(limit - given[i], max(1, remaining * weights[i] // mass), spare)
            given[i] = given[i] + addition
            spare = spare - addition
    return np.array(given)


def normal_values(rng, extent, width, reach, cuts=(), kind=jnp.bfloat16):
    values = width * jax.random.normal(rng, extent, jnp.float32)
    if cuts:
        values = values * level_of(rng, extent, cuts, -0.22, 0.18)
    return jnp.clip(values, -reach, reach).astype(kind)


def heavy_noise(key, dims, deviation, reach, cuts, heavy, kind=jnp.bfloat16):
    array = deviation * jax.random.normal(key, dims, jnp.float32)
    if cuts:
        array = array * level_of(key, dims, cuts, -0.22, 0.18)
    return jnp.clip(strengthened(array, jax.random.fold_in(key, 3), *heavy), -reach, reach).astype(kind)


def setup_inputs(seed: int = 0) -> dict:
    streams_of = jax.random.split(jax.random.key(seed), 6)
    grad_out = heavy_noise(streams_of[0], (TOKENS, D), 1.0, 6.0, ((0, 32),), (0, 1, 32, 2.75))
    saved_pre = normal_values(streams_of[1], (TOKENS, TOP, 2 * HID), 1.0, 6.0, ((0, 32),))
    gate_probs = jnp.clip(0.019897461 + 0.17932129 * jax.random.uniform(streams_of[2], (TOKENS, TOP), jnp.float32) ** level_of(streams_of[2], (TOKENS, TOP), ((0, 32),), -0.2, 0.2), 0.019897461, 0.19921875).astype(jnp.bfloat16)
    routes_keys = jax.random.split(jax.random.fold_in(streams_of[3], 1), TOKENS // TOK_DEV)
    routes_turns = jax.random.permutation(jax.random.fold_in(streams_of[3], 3), TOKENS // TOK_DEV)
    routes = jax.vmap(lambda own, number: shared_out(jax.random.fold_in(streams_of[3], 2), own, number, TOK_DEV, EXPERTS, TOP, CAP, 2))(routes_keys, routes_turns).reshape((TOKENS, TOP))
    down_weight = normal_values(streams_of[4], (EXPERTS, HID, D), D ** -0.5, 0.125, ((0, 8),))
    return dict(grad_out=grad_out, saved_pre=saved_pre, gate_probs=gate_probs, routes=routes, down_weight=down_weight)


def swiglu_back(pre, grad_hid):
    gate_pre = pre[..., :HID].astype(jnp.float32)
    up_pre = pre[..., HID:].astype(jnp.float32)
    sigmoid_a = jax.nn.sigmoid(gate_pre)
    silu_gate = gate_pre * sigmoid_a
    grad_wide = grad_hid.astype(jnp.float32)
    gate_grad = grad_wide * up_pre * sigmoid_a * (1.0 + gate_pre * (1.0 - sigmoid_a))
    up_grad = grad_wide * silu_gate
    return jnp.concatenate([gate_grad, up_grad], -1).astype(jnp.bfloat16)


def with_zero(values):
    return jnp.concatenate([values, jnp.zeros((1,) + values.shape[1:], values.dtype)], 0)


def reference(grad_out, saved_pre, gate_probs, routes, down_weight):
    row_tokens = TOK_DEV * N_EXPERT
    slot_count = row_tokens * TOP
    table_width = N_EXPERT * CAP
    weight_wide = down_weight.astype(jnp.float32)

    def one_row(total, inputs):
        grad_rows, pre_rows, prob_rows, route_rows = inputs
        flat_ids = route_rows.reshape(slot_count).astype(jnp.int32)
        sort_order = jnp.argsort(flat_ids, stable=True).astype(jnp.int32)
        sorted_ids = flat_ids[sort_order]
        onehot = (flat_ids[:, None] == jnp.arange(EXPERTS, dtype=jnp.int32)[None, :]).astype(jnp.int32)
        counts = jnp.sum(onehot, 0).astype(jnp.int32)
        starts = (jnp.cumsum(counts) - counts).astype(jnp.int32)
        places = jnp.arange(slot_count, dtype=jnp.int32) - starts[sorted_ids]
        slot_table = jnp.full((EXPERTS, table_width), slot_count, jnp.int32).at[sorted_ids, places].set(sort_order)
        pre_flat = pre_rows.reshape(slot_count, 2 * HID)
        gate_pre = pre_flat[:, :HID].astype(jnp.float32)
        hidden = (jax.nn.silu(gate_pre) * pre_flat[:, HID:].astype(jnp.float32)).astype(jnp.bfloat16)
        prob_flat = prob_rows.reshape(slot_count).astype(jnp.float32)
        token_of = jnp.arange(slot_count, dtype=jnp.int32) // TOP
        grad_flat = grad_rows[token_of]
        scaled = (prob_flat[:, None] * grad_flat.astype(jnp.float32)).astype(jnp.bfloat16)
        grad_table = with_zero(grad_flat)[slot_table]
        hidden_table = with_zero(hidden)[slot_table]
        prob_table = with_zero(prob_flat)[slot_table]
        scaled_table = with_zero(scaled)[slot_table]
        projected = jnp.einsum("emd,ehd->emh", grad_table.astype(jnp.float32), weight_wide)
        grad_prob_table = jnp.sum(projected * hidden_table.astype(jnp.float32), -1)
        grad_hid_table = (prob_table[..., None] * projected).astype(jnp.bfloat16)
        partial_value = jnp.einsum("emh,emd->ehd", hidden_table.astype(jnp.float32), scaled_table.astype(jnp.float32))
        rounded = lax.optimization_barrier(partial_value.astype(jnp.bfloat16))
        total = total + rounded.astype(jnp.float32)
        grad_hid_slots = jnp.zeros((slot_count + 1, HID), jnp.bfloat16).at[slot_table].set(grad_hid_table)[:slot_count]
        grad_prob_slots = jnp.zeros((slot_count + 1,), jnp.float32).at[slot_table].set(grad_prob_table)[:slot_count]
        grad_pre_rows = swiglu_back(pre_flat, grad_hid_slots).reshape(row_tokens, TOP, 2 * HID)
        grad_prob_rows = grad_prob_slots.astype(jnp.bfloat16).reshape(row_tokens, TOP)
        return total, (grad_pre_rows, grad_prob_rows)

    inputs = (grad_out.reshape(N_DP, row_tokens, D),
              saved_pre.reshape(N_DP, row_tokens, TOP, 2 * HID),
              gate_probs.reshape(N_DP, row_tokens, TOP),
              routes.reshape(N_DP, row_tokens, TOP))
    start_total = jnp.zeros((EXPERTS, HID, D), jnp.float32)
    total, (grad_pre, grad_probs) = lax.scan(one_row, start_total, inputs)
    grad_pre = grad_pre.reshape(TOKENS, TOP, 2 * HID)
    grad_probs = grad_probs.reshape(TOKENS, TOP)
    return grad_pre, grad_probs, total.astype(jnp.bfloat16)
```

```python
import functools
import math

import jax
import jax.numpy as jnp
from jax import lax
from jax.experimental import pallas as pl
from jax.experimental.pallas import tpu as pltpu
from jax.sharding import PartitionSpec as P

LANES = 128
MIB = 1024 * 1024
ANY = pl.BlockSpec(memory_space=pl.ANY)
VMEM = pl.BlockSpec(memory_space=pltpu.VMEM)
SMEM = pl.BlockSpec(memory_space=pltpu.SMEM)


def call(kernel, outs, operands, specs, scratch=(), mib=12):
    return pl.pallas_call(
        kernel,
        out_shape=outs,
        in_specs=specs,
        out_specs=[VMEM] * len(outs) if isinstance(outs, list) else VMEM,
        scratch_shapes=list(scratch),
        compiler_params=pltpu.CompilerParams(vmem_limit_bytes=mib * MIB),
    )(*operands)


def shape(*dims):
    return jax.ShapeDtypeStruct(dims, jnp.bfloat16)


def fetch(sources, first, width, stage, sems, start_row=0, start_sem=0):
    copies, at = [], start_row
    for i, source in enumerate(sources):
        rows = source.shape[0]
        copy = pltpu.make_async_copy(
            source.at[:, pl.ds(first, width)], stage.at[pl.ds(at, rows), :], sems.at[start_sem + i]
        )
        copy.start()
        copies.append(copy)
        at += rows
    return copies


def in_hbm(values):
    return pltpu.with_memory_space_constraint(values, pltpu.HBM)


def send(values, axis, pairs):
    return in_hbm(lax.ppermute(values, axis, pairs))


def swap(values, axis, size, offset):
    return send(values, axis, [(i, i ^ offset) for i in range(size)])


def gather_rows(block, *hold):
    straight = [(i, i ^ (4 if i % 2 else 2)) for i in range(8)]
    crosswise = [(i, i ^ (2 if i % 2 else 4)) for i in range(8)]
    sibling = swap(block, "expert", 8, 1)
    first = send(block, "expert", straight)
    second = send(sibling, "expert", straight)
    corner = send(first, "expert", crosswise)
    passed = after((first, second, corner), *hold) if hold else (first, second, corner)
    return [block, sibling, first, second, corner] + [swap(v, "expert", 8, 1) for v in passed]


def block_offsets(me):
    straight = jnp.where(me % 2 == 0, 2, 4).astype(jnp.int32)
    crosswise = 6 - straight
    return [0, 1, straight, straight + 1, 6, crosswise + 1, crosswise, 7]


def after(values, *others):
    return lax.optimization_barrier((*values, *others))[: len(values)]


def lead_kernel(units, width, plan_ref, *refs):
    pre_hbm, probs_hbm, names_hbm, grad_ref, own_ref, near_ref, rest_ref, keep_ref = refs[:8]
    pre_ref, probs_ref, names_ref, sems = refs[8:]
    tokens = own_ref.shape[0]
    used = 2 * units + LANES
    inputs = []
    for i, pair in enumerate(((names_hbm, names_ref), (probs_hbm, probs_ref), (pre_hbm, pre_ref))):
        inputs.append(pltpu.make_async_copy(*pair, sems.at[6 + i]))
        inputs[-1].start()
    targets = [
        own_ref.at[:, pl.ds(used, width)],
        near_ref.at[:, pl.ds(used, width)],
        keep_ref.at[:, pl.ds(0, width)],
    ] + [rest_ref.at[:, pl.ds(i * width, width)] for i in range(3)]
    copies = []
    for i, target in enumerate(targets):
        at = pl.multiple_of(plan_ref[i] * width, LANES)
        copies.append(pltpu.make_async_copy(grad_ref.at[:, pl.ds(at, width)], target, sems.at[i]))
        copies[-1].start()
    for copy in inputs:
        copy.wait()
    probs = probs_ref[...].astype(jnp.float32).T
    names = names_ref[...].astype(jnp.float32).T
    for k in range(2):
        gate = pre_ref[:, k, :units].astype(jnp.float32)
        up = pre_ref[:, k, units:].astype(jnp.float32)
        hidden = (gate * jax.nn.sigmoid(gate) * up).astype(jnp.bfloat16).astype(jnp.float32)
        scaled = (hidden * probs[:, k : k + 1]).astype(jnp.bfloat16)
        own_ref[:, k * units : (k + 1) * units] = scaled
        near_ref[:, k * units : (k + 1) * units] = scaled
    lane = lax.broadcasted_iota(jnp.int32, (tokens, LANES), 1)
    wide = jnp.where(lane == 0, names[:, 0:1], jnp.where(lane == 1, names[:, 1:2], 0.0)).astype(jnp.bfloat16)
    own_ref[:, 2 * units : used] = wide
    near_ref[:, 2 * units : used] = wide
    for copy in copies:
        copy.wait()


def masked(stage, out_ref, units, per_device, tokens, base):
    for d in range(stage.shape[0] // tokens):
        rows = pl.ds(d * tokens, tokens)
        names = stage[rows, 2 * units : 2 * units + LANES].astype(jnp.float32)
        values = [stage[rows, k * units : (k + 1) * units].astype(jnp.float32) for k in range(2)]
        for j in range(per_device):
            expert = (base + j).astype(jnp.float32)
            part = jnp.zeros((tokens, units), jnp.float32)
            for k in range(2):
                part = part + jnp.where(names[:, k : k + 1] == expert, values[k], 0.0)
            out_ref[j * units : (j + 1) * units, d * tokens : (d + 1) * tokens] = part.T.astype(jnp.bfloat16)


def times_weight(rows, weight):
    return lax.dot_general(rows, weight, (((1,), (1,)), ((), ())), preferred_element_type=jnp.float32)


def wait_all(copies):
    for copy in copies:
        copy.wait()


def own_first_kernel(units, per_device, tokens, count, width, capacity, plan_ref, weight_hbm, *refs):
    sources = refs[:count]
    hidden_ref, given_ref, total_ref, chosen_ref, stage, weight, sems = refs[count:]
    used = 2 * units + LANES
    at = pl.multiple_of(plan_ref[0] * width, LANES)
    loaded = pltpu.make_async_copy(weight_hbm.at[:, pl.ds(at, width)], weight, sems.at[count])
    copies = fetch(sources, 0, used + width, stage, sems)
    loaded.start()
    wait_all(copies)
    base = plan_ref[4]
    masked(stage, hidden_ref, units, per_device, tokens, base)
    given_ref[...] = jnp.dot(hidden_ref[...], stage[:, used:], preferred_element_type=jnp.float32)
    loaded.wait()
    total_ref[...] = times_weight(stage[:, used:], weight[...])
    lane = lax.broadcasted_iota(jnp.int32, (tokens, LANES), 1)
    row = lax.broadcasted_iota(jnp.int32, (tokens, tokens), 0)
    col = lax.broadcasted_iota(jnp.int32, (tokens, tokens), 1)
    earlier = (row > col).astype(jnp.bfloat16)
    expert = (base + lane // capacity).astype(jnp.float32)
    place = (lane % capacity).astype(jnp.float32)
    span = per_device * capacity
    usable = lane < span
    for d in range(stage.shape[0] // tokens):
        names = stage[pl.ds(d * tokens, tokens), 2 * units : used].astype(jnp.float32)
        named = ((names[:, 0:1] == expert) | (names[:, 1:2] == expert)) & usable
        rank = jnp.dot(earlier, named.astype(jnp.bfloat16), preferred_element_type=jnp.float32)
        chosen = jnp.where(named & (rank == place), 1.0, 0.0).T.astype(jnp.bfloat16)
        chosen_ref[d * span : (d + 1) * span, :] = chosen[:span, :]


def near_first_kernel(units, per_device, tokens, count, width, plan_ref, given_ref, *refs):
    sources = refs[:count]
    hidden_ref, out_ref, stage, sems = refs[count:]
    used = 2 * units + LANES
    wait_all(fetch(sources, 0, used + width, stage, sems))
    masked(stage, hidden_ref, units, per_device, tokens, plan_ref[4])
    part = jnp.dot(hidden_ref[...], stage[:, used:], preferred_element_type=jnp.float32)
    out_ref[...] = (given_ref[...] + part).astype(jnp.bfloat16)


def own_rest_kernel(units, per_device, tokens, count, width, capacity, pieces, plan_ref, weight_hbm, *refs):
    hidden_ref, total_ref, chosen_ref = refs[:3]
    sources = refs[3 : 3 + count]
    packed_ref, kept_ref, stage, weight, sems = refs[3 + count :]
    copies = fetch(sources, 0, 3 * width, stage, sems)
    loads = []
    for q in range(3):
        at = pl.multiple_of(plan_ref[1 + q] * width, LANES)
        loads.append(
            pltpu.make_async_copy(
                weight_hbm.at[:, pl.ds(at, width)], weight.at[:, pl.ds(q * width, width)], sems.at[count + q]
            )
        )
        loads[-1].start()
    wait_all(loads)
    wait_all(copies)
    span = per_device * capacity
    blocks = stage.shape[0] // tokens
    step = 4 if blocks % 4 == 0 else 1
    for d0 in range(0, blocks, step):
        rows = pl.ds(d0 * tokens, step * tokens)
        projected = (total_ref[rows, :] + times_weight(stage[rows, :], weight[...])).astype(jnp.bfloat16)
        for d in range(d0, d0 + step):
            packed = jnp.dot(
                chosen_ref[d * span : (d + 1) * span, :],
                projected[(d - d0) * tokens : (d - d0 + 1) * tokens, :],
                preferred_element_type=jnp.float32,
            )
            to = pl.multiple_of(plan_ref[5 + d] * span, 8)
            block = jnp.concatenate(
                [
                    packed[j * capacity : (j + 1) * capacity, j * units : (j + 1) * units]
                    for j in range(per_device)
                ],
                0,
            )
            packed_ref[pl.ds(to, span), :] = block.astype(jnp.bfloat16)
    for q in range(pieces):
        kept_ref[:, q * width : (q + 1) * width] = jnp.dot(
            hidden_ref[...], stage[:, q * width : (q + 1) * width], preferred_element_type=jnp.float32
        )


def near_rest_kernel(count, hidden_ref, kept_ref, *refs):
    sources = refs[:count]
    out_ref, stage, sems = refs[count:]
    wait_all(fetch(sources, 0, stage.shape[1], stage, sems))
    out_ref[...] = kept_ref[...] + jnp.dot(hidden_ref[...], stage[...], preferred_element_type=jnp.float32)


def finish_kernel(units, capacity, names_ref, pre_ref, probs_ref, packed_ref, grad_ref, grad_probs_ref):
    tokens = names_ref.shape[1]
    slots = packed_ref.shape[0]
    experts = slots // capacity
    e_lane = lax.broadcasted_iota(jnp.int32, (tokens, experts), 1).astype(jnp.float32)
    row = lax.broadcasted_iota(jnp.int32, (tokens, tokens), 0)
    col = lax.broadcasted_iota(jnp.int32, (tokens, tokens), 1)
    earlier = (row > col).astype(jnp.bfloat16)
    names = names_ref[...].astype(jnp.float32).T
    hits = [names[:, k : k + 1] == e_lane for k in range(2)]
    rank = jnp.dot(earlier, (hits[0] | hits[1]).astype(jnp.bfloat16), preferred_element_type=jnp.float32)
    lane = lax.broadcasted_iota(jnp.int32, (tokens, slots), 1).astype(jnp.float32)
    probs = probs_ref[...].astype(jnp.float32).T
    sums = []
    for k in range(2):
        mine = jnp.sum(jnp.where(hits[k], rank, 0.0), axis=1, keepdims=True)
        chosen = (lane == names[:, k : k + 1] * capacity + mine).astype(jnp.bfloat16)
        projected = jnp.dot(chosen, packed_ref[...], preferred_element_type=jnp.float32)
        gate = pre_ref[:, k, :units].astype(jnp.float32)
        up = pre_ref[:, k, units:].astype(jnp.float32)
        sigmoid = jax.nn.sigmoid(gate)
        silu = gate * sigmoid
        hidden = (silu * up).astype(jnp.bfloat16).astype(jnp.float32)
        sums.append(jnp.sum(projected * hidden, axis=1, keepdims=True))
        wide = (probs[:, k : k + 1] * projected).astype(jnp.bfloat16).astype(jnp.float32)
        grad_ref[:, k, :units] = (wide * up * sigmoid * (1.0 + gate * (1.0 - sigmoid))).astype(jnp.bfloat16)
        grad_ref[:, k, units:] = (wide * silu).astype(jnp.bfloat16)
    pair = lax.broadcasted_iota(jnp.int32, (tokens, LANES), 1)
    both = jnp.where(pair == 0, sums[0], jnp.where(pair == 1, sums[1], 0.0))
    grad_probs_ref[...] = both.T[:2, :].astype(jnp.bfloat16)


def add_kernel(a_ref, b_ref, out_ref):
    out_ref[...] = (a_ref[...].astype(jnp.float32) + b_ref[...].astype(jnp.float32)).astype(jnp.bfloat16)


def local(grad_out, saved_pre, gate_probs, routes, down_weight):
    devices = lax.axis_size("expert")
    planes = lax.axis_size("dp")
    per_device, units, model_width = down_weight.shape
    tokens, per_token = routes.shape
    experts = per_device * devices
    capacity = 2 * tokens * per_token // experts
    me = lax.axis_index("expert").astype(jnp.int32)
    plane = lax.axis_index("dp").astype(jnp.int32)
    paired = planes == 4 and devices == 8
    width = model_width // 4
    used = per_token * units + LANES
    held = per_device * units
    everyone = devices * tokens

    if paired:
        near = plane ^ 1
        give, keep = 3 - plane, plane
        order = [give, 3 - near, keep, keep, 3 - near, near]
        order[1] = 3 - near
        sends = [give, 3 - near, near, keep, 3 - near, near]
    else:
        sends = [jnp.int32(i) for i in (0, 0, 0, 1, 2, 3)]
    plan = jnp.stack(sends).astype(jnp.int32)

    def staged(rows, columns):
        return pltpu.VMEM((rows, columns), jnp.bfloat16)

    lead, near_lead, rest, near_keep = call(
        functools.partial(lead_kernel, units, width),
        [
            shape(tokens, used + width),
            shape(tokens, used + width),
            shape(tokens, 3 * width),
            shape(tokens, width),
        ],
        [plan] + [in_hbm(v) for v in (saved_pre, gate_probs.T, routes.T, grad_out)],
        [SMEM] + [ANY] * 4,
        [
            pltpu.VMEM(saved_pre.shape, jnp.bfloat16),
            pltpu.VMEM((per_token, tokens), jnp.bfloat16),
            pltpu.VMEM((per_token, tokens), jnp.int32),
            pltpu.SemaphoreType.DMA((9,)),
        ],
    )

    def first(sources, plan):
        rows = sum(source.shape[0] for source in sources)
        return call(
            functools.partial(own_first_kernel, units, per_device, tokens, len(sources), width, capacity),
            [
                shape(held, rows),
                jax.ShapeDtypeStruct((held, width), jnp.float32),
                jax.ShapeDtypeStruct((rows, held), jnp.float32),
                shape(rows // tokens * per_device * capacity, LANES),
            ],
            [plan, weight] + sources,
            [SMEM] + [ANY] * (1 + len(sources)),
            [staged(rows, used + width), staged(held, width), pltpu.SemaphoreType.DMA((len(sources) + 1,))],
            mib=20,
        )

    def last(hidden, total, chosen, sources, plan, pieces):
        rows = sum(source.shape[0] for source in sources)
        return call(
            functools.partial(
                own_rest_kernel, units, per_device, tokens, len(sources), width, capacity, pieces
            ),
            [
                shape(rows // tokens * per_device * capacity, units),
                jax.ShapeDtypeStruct((held, pieces * width), jnp.float32),
            ],
            [plan, weight, hidden, total, chosen] + sources,
            [SMEM, ANY] + [VMEM] * 3 + [ANY] * len(sources),
            [staged(rows, 3 * width), staged(held, 3 * width), pltpu.SemaphoreType.DMA((len(sources) + 3,))],
            mib=24,
        )

    weight = in_hbm(down_weight.reshape(held, model_width))
    base = me * per_device
    if paired:
        plan = jnp.stack(
            [give, keep, 3 - near, near, base] + [me ^ offset for offset in block_offsets(me)]
        ).astype(jnp.int32)
        near_lead = swap(near_lead, "dp", 4, 1)
        near_keep = swap(near_keep, "dp", 4, 1)
        own_first = gather_rows(lead)
        hidden, given, total, chosen = first(own_first, plan)
        near_lead = after((near_lead,), own_first[3])[0]
        near_first = gather_rows(near_lead, given)
        near_hidden, given = call(
            functools.partial(near_first_kernel, units, per_device, tokens, len(near_first), width),
            [shape(held, everyone), shape(held, width)],
            [plan, given] + near_first,
            [SMEM, VMEM] + [ANY] * len(near_first),
            [staged(everyone, used + width), pltpu.SemaphoreType.DMA((len(near_first),))],
            mib=16,
        )
        crossed = lax.ppermute(given, "dp", [(0, 3), (3, 0), (1, 2), (2, 1)])
        rest, near_keep = after((rest, near_keep), *near_first[3:5])
        own_rest = gather_rows(rest)
        near_keep = after((near_keep,), *own_rest[3:5])[0]
        near_rest = gather_rows(near_keep)
        packed, kept = last(hidden, total, chosen, own_rest, plan, 1)
        kept = call(
            functools.partial(near_rest_kernel, len(near_rest)),
            jax.ShapeDtypeStruct((held, width), jnp.float32),
            [near_hidden, kept] + near_rest,
            [VMEM] * 2 + [ANY] * len(near_rest),
            [staged(everyone, width), pltpu.SemaphoreType.DMA((len(near_rest),))],
        )
        summed = call(add_kernel, shape(held, width), [kept, crossed], [VMEM, VMEM])
    else:
        own_first = lax.all_gather(lead, "expert", axis=0, tiled=True)
        own_rest = lax.all_gather(rest, "expert", axis=0, tiled=True)
        group = math.gcd(devices, 8)
        plan = jnp.concatenate(
            [jnp.arange(4, dtype=jnp.int32), base.reshape(1), jnp.arange(group, dtype=jnp.int32)]
        )
        partial, packs = 0.0, []
        for i in range(0, devices, group):
            rows = slice(i * tokens, (i + group) * tokens)
            hidden, given, total, chosen = first([own_first[rows]], plan)
            packed, kept = last(hidden, total, chosen, [own_rest[rows]], plan, 3)
            partial = partial + jnp.concatenate([given, kept], 1)
            packs.append(packed)
        packed = jnp.concatenate(packs, 0)
        summed = lax.psum_scatter(partial.astype(jnp.bfloat16), "dp", scatter_dimension=1, tiled=True)

    returned = lax.all_to_all(packed, "expert", 0, 0, tiled=True)
    grad_pre, grad_probs = call(
        functools.partial(finish_kernel, units, capacity),
        [shape(tokens, per_token, 2 * units), shape(per_token, tokens)],
        [routes.T, saved_pre, gate_probs.T, returned],
        [VMEM] * 4,
    )
    return grad_pre, grad_probs.T, summed.reshape(per_device, units, model_width // planes)


def solution(mesh):
    in_specs = (
        P(("dp", "expert"), None),
        P(("dp", "expert"), None, None),
        P(("dp", "expert"), None),
        P(("dp", "expert"), None),
        P("expert", None, None),
    )
    out_specs = (
        P(("dp", "expert"), None, None),
        P(("dp", "expert"), None),
        P("expert", None, "dp"),
    )
    return jax.shard_map(local, mesh=mesh, in_specs=in_specs, out_specs=out_specs, check_vma=False)
```

```python
import functools
import math

import jax
import jax.numpy as jnp
from jax import lax
from jax.experimental import pallas as pl
from jax.experimental.pallas import tpu as pltpu
from jax.sharding import PartitionSpec as P

LANES = 128
MIB = 1024 * 1024
ANY = pl.BlockSpec(memory_space=pl.ANY)
VMEM = pl.BlockSpec(memory_space=pltpu.VMEM)
SMEM = pl.BlockSpec(memory_space=pltpu.SMEM)


def call(kernel, outs, operands, specs, scratch=(), mib=12, flops=0, out_specs=None):
    arrays = list(operands) + (outs if isinstance(outs, list) else [outs])
    moved = sum(math.prod(v.shape) * jnp.dtype(v.dtype).itemsize for v in arrays)
    return pl.pallas_call(
        kernel,
        out_shape=outs,
        in_specs=specs,
        out_specs=out_specs or ([VMEM] * len(outs) if isinstance(outs, list) else VMEM),
        scratch_shapes=list(scratch),
        compiler_params=pltpu.CompilerParams(vmem_limit_bytes=mib * MIB),
        cost_estimate=pl.CostEstimate(flops=flops, transcendentals=0, bytes_accessed=moved),
    )(*operands)


def shape(*dims):
    return jax.ShapeDtypeStruct(dims, jnp.bfloat16)


def fetch(sources, first, width, stage, sems, start_row=0, start_sem=0):
    copies, at = [], start_row
    for i, source in enumerate(sources):
        rows = source.shape[0]
        copy = pltpu.make_async_copy(
            source.at[:, pl.ds(first, width)], stage.at[pl.ds(at, rows), :], sems.at[start_sem + i]
        )
        copy.start()
        copies.append(copy)
        at += rows
    return copies


def in_hbm(values):
    return pltpu.with_memory_space_constraint(values, pltpu.HBM)


def in_vmem(values):
    return pltpu.with_memory_space_constraint(values, pltpu.VMEM)


def send(values, axis, pairs, place=in_vmem):
    return place(lax.ppermute(values, axis, pairs))


def swap(values, axis, size, offset, place=in_vmem):
    return send(values, axis, [(i, i ^ offset) for i in range(size)], place)


STRAIGHT = [(i, i ^ (4 if i % 2 else 2)) for i in range(8)]
CROSSWISE = [(i, i ^ (2 if i % 2 else 4)) for i in range(8)]


def gather_rows(block, corner_hold=(), back=((), (), ()), in_turn=False, place=in_vmem):
    sibling = swap(block, "expert", 8, 1, place)
    first = send(block, "expert", STRAIGHT, place)
    second = send(sibling, "expert", STRAIGHT, place)
    hold = (*corner_hold, second) if in_turn else corner_hold
    corner = send(after((first,), *hold)[0], "expert", CROSSWISE, place)
    places = (place, in_vmem, in_vmem)
    over = [
        swap(after((v,), *holds)[0], "expert", 8, 1, last)
        for v, holds, last in zip((first, second, corner), back, places)
    ]
    return [block, sibling, first, second, corner] + over


def block_offsets(me):
    straight = jnp.where(me % 2 == 0, 2, 4).astype(jnp.int32)
    crosswise = 6 - straight
    return [0, 1, straight, straight + 1, 6, crosswise + 1, crosswise, 7]


def after(values, *others):
    return lax.optimization_barrier((*values, *others))[: len(values)] if others else values


def lead_kernel(units, width, plan_ref, *refs):
    pre_hbm, probs_hbm, names_hbm, grad_ref, own_ref, near_ref, rest_ref, keep_ref = refs[:8]
    pre_ref, probs_ref, names_ref, sems = refs[8:]
    tokens = own_ref.shape[0]
    used = 2 * units + LANES
    inputs = []
    for i, pair in enumerate(((names_hbm, names_ref), (probs_hbm, probs_ref), (pre_hbm, pre_ref))):
        inputs.append(pltpu.make_async_copy(*pair, sems.at[6 + i]))
        inputs[-1].start()
    targets = [
        own_ref.at[:, pl.ds(used, width)],
        near_ref.at[:, pl.ds(used, width)],
        keep_ref.at[:, pl.ds(0, width)],
    ] + [rest_ref.at[:, pl.ds(i * width, width)] for i in range(3)]
    copies = []
    for i, target in enumerate(targets):
        at = pl.multiple_of(plan_ref[i] * width, LANES)
        copies.append(pltpu.make_async_copy(grad_ref.at[:, pl.ds(at, width)], target, sems.at[i]))
        copies[-1].start()
    for copy in inputs:
        copy.wait()
    probs = probs_ref[...].astype(jnp.float32).T
    names = names_ref[...].astype(jnp.float32).T
    for k in range(2):
        gate = pre_ref[:, k, :units].astype(jnp.float32)
        up = pre_ref[:, k, units:].astype(jnp.float32)
        hidden = (gate * jax.nn.sigmoid(gate) * up).astype(jnp.bfloat16).astype(jnp.float32)
        scaled = (hidden * probs[:, k : k + 1]).astype(jnp.bfloat16)
        own_ref[:, k * units : (k + 1) * units] = scaled
        near_ref[:, k * units : (k + 1) * units] = scaled
    lane = lax.broadcasted_iota(jnp.int32, (tokens, LANES), 1)
    wide = jnp.where(lane == 0, names[:, 0:1], jnp.where(lane == 1, names[:, 1:2], 0.0)).astype(jnp.bfloat16)
    own_ref[:, 2 * units : used] = wide
    near_ref[:, 2 * units : used] = wide
    for copy in copies:
        copy.wait()


def masked(stage, out_ref, units, per_device, tokens, base):
    for d in range(stage.shape[0] // tokens):
        rows = pl.ds(d * tokens, tokens)
        names = stage[rows, 2 * units : 2 * units + LANES].astype(jnp.float32)
        values = [stage[rows, k * units : (k + 1) * units].astype(jnp.float32) for k in range(2)]
        for j in range(per_device):
            expert = (base + j).astype(jnp.float32)
            part = jnp.zeros((tokens, units), jnp.float32)
            for k in range(2):
                part = part + jnp.where(names[:, k : k + 1] == expert, values[k], 0.0)
            out_ref[j * units : (j + 1) * units, d * tokens : (d + 1) * tokens] = part.T.astype(jnp.bfloat16)


def times_weight(rows, weight):
    return lax.dot_general(rows, weight, (((1,), (1,)), ((), ())), preferred_element_type=jnp.float32)


def wait_all(copies):
    for copy in copies:
        copy.wait()


def turn_kernel(width, plan_ref, weight_hbm, out_ref, weight, sems):
    loads = []
    for q in range(3):
        at = pl.multiple_of(plan_ref[q + 1] * width, LANES)
        loads.append(pltpu.make_async_copy(weight_hbm.at[:, pl.ds(at, width)], weight.at[q], sems.at[q]))
        loads[-1].start()
    for q in range(3):
        loads[q].wait()
        out_ref[q * width : (q + 1) * width, :] = weight[q].T


def early_kernel(units, per_device, tokens, count, width, capacity, plan_ref, weight_hbm, *refs):
    sources = refs[:count]
    total_ref, chosen_ref, stage, weight, picked, sems = refs[count:]
    at = pl.multiple_of(plan_ref[0] * width, LANES)
    loaded = pltpu.make_async_copy(weight_hbm.at[:, pl.ds(at, width)], weight, sems.at[count])
    loaded.start()
    wait_all(fetch(sources, 2 * units, LANES + width, stage, sems))
    lane = lax.broadcasted_iota(jnp.int32, (tokens, LANES), 1)
    row = lax.broadcasted_iota(jnp.int32, (tokens, tokens), 0)
    col = lax.broadcasted_iota(jnp.int32, (tokens, tokens), 1)
    earlier = (row > col).astype(jnp.bfloat16)
    expert = (plan_ref[4] + lane // capacity).astype(jnp.float32)
    place = (lane % capacity).astype(jnp.float32)
    span = per_device * capacity
    usable = lane < span
    blocks = stage.shape[0] // tokens
    for d in range(blocks):
        rows = pl.ds(d * tokens, tokens)
        names = stage[rows, :LANES].astype(jnp.float32)
        named = ((names[:, 0:1] == expert) | (names[:, 1:2] == expert)) & usable
        rank = jnp.dot(earlier, named.astype(jnp.bfloat16), preferred_element_type=jnp.float32)
        chosen = jnp.where(named & (rank == place), 1.0, 0.0).T.astype(jnp.bfloat16)
        chosen_ref[d * span : (d + 1) * span, :] = chosen[:span, :]
        pick(chosen[:span, :], stage[rows, LANES:], picked, d, blocks, capacity)
    loaded.wait()
    for j in range(per_device):
        rows = pl.ds(j * blocks * capacity, blocks * capacity)
        total_ref[rows, :] = times_weight(picked[rows, :].astype(jnp.bfloat16), weight[j * units : (j + 1) * units, :])


def pick(chosen, values, picked, d, blocks, capacity):
    rows = jnp.dot(chosen, values, preferred_element_type=jnp.float32)
    for j in range(chosen.shape[0] // capacity):
        picked[pl.ds((j * blocks + d) * capacity, capacity), :] = rows[j * capacity : (j + 1) * capacity, :]


def first_kernel(units, per_device, tokens, count, width, started, plan_ref, *refs):
    sources = refs[started : started + count]
    hidden_hbm, *out_refs, hidden_ref, stage, sems = refs[started + count :]
    used = 2 * units + LANES
    wait_all(fetch(sources, 0, used + width, stage, sems))
    masked(stage, hidden_ref, units, per_device, tokens, plan_ref[4])
    stored = pltpu.make_async_copy(hidden_ref, hidden_hbm, sems.at[count])
    stored.start()
    part = jnp.dot(hidden_ref[...], stage[:, used:], preferred_element_type=jnp.float32)
    part = part + refs[0][...] if started else part
    at = 0
    for out_ref in out_refs:
        out_ref[...] = part[at : at + out_ref.shape[0], :].astype(out_ref.dtype)
        at += out_ref.shape[0]
    stored.wait()


def project_kernel(units, per_device, tokens, count, width, capacity, plan_ref, *refs):
    total_ref, chosen_ref, weight = refs[:3]
    sources = refs[3 : 3 + count]
    packed_ref, stage, picked, sems = refs[3 + count :]
    wait_all(fetch(sources, 0, 3 * width, stage, sems))
    span = per_device * capacity
    blocks = stage.shape[0] // tokens
    for d in range(blocks):
        pick(
            chosen_ref[d * span : (d + 1) * span, :],
            stage[pl.ds(d * tokens, tokens), :],
            picked,
            d,
            blocks,
            capacity,
        )
    projected = []
    for j in range(per_device):
        rows = pl.ds(j * blocks * capacity, blocks * capacity)
        part = jnp.dot(
            picked[rows, :].astype(jnp.bfloat16),
            weight[:, j * units : (j + 1) * units],
            preferred_element_type=jnp.float32,
        )
        projected.append(total_ref[rows, :] + part)
    for d in range(blocks):
        to = pl.multiple_of(plan_ref[5 + d] * span, 8)
        block = jnp.concatenate([values[d * capacity : (d + 1) * capacity, :] for values in projected], 0)
        packed_ref[pl.ds(to, span), :] = block.astype(jnp.bfloat16)


def columns_kernel(parts, width, *refs):
    at = len(parts)
    out_ref, hidden_ref, stage, sems = refs[-4:]
    waits, row, sem = [], 0, 0
    for i, (count, first) in enumerate(parts):
        sources = refs[at : at + count]
        rows = sum(source.shape[0] for source in sources)
        copies = fetch(sources, first, width, stage, sems, row, sem)
        copies.append(
            pltpu.make_async_copy(refs[i], hidden_ref.at[:, pl.ds(row, rows)], sems.at[sem + count])
        )
        copies[-1].start()
        waits.append((pl.ds(row, rows), copies))
        row += rows
        sem += count + 1
        at += count
    for i, (rows, copies) in enumerate(waits):
        wait_all(copies)
        part = jnp.dot(hidden_ref[:, rows], stage[rows, :], preferred_element_type=jnp.float32)
        out_ref[...] = part if i == 0 else out_ref[...] + part


def finish_kernel(units, capacity, names_ref, pre_ref, probs_ref, packed_ref, grad_ref, grad_probs_ref):
    tokens = names_ref.shape[1]
    slots = packed_ref.shape[0]
    experts = slots // capacity
    e_lane = lax.broadcasted_iota(jnp.int32, (tokens, experts), 1).astype(jnp.float32)
    row = lax.broadcasted_iota(jnp.int32, (tokens, tokens), 0)
    col = lax.broadcasted_iota(jnp.int32, (tokens, tokens), 1)
    earlier = (row > col).astype(jnp.bfloat16)
    names = names_ref[...].astype(jnp.float32).T
    hits = [names[:, k : k + 1] == e_lane for k in range(2)]
    rank = jnp.dot(earlier, (hits[0] | hits[1]).astype(jnp.bfloat16), preferred_element_type=jnp.float32)
    lane = lax.broadcasted_iota(jnp.int32, (tokens, slots), 1).astype(jnp.float32)
    probs = probs_ref[...].astype(jnp.float32).T
    sums = []
    for k in range(2):
        mine = jnp.sum(jnp.where(hits[k], rank, 0.0), axis=1, keepdims=True)
        chosen = (lane == names[:, k : k + 1] * capacity + mine).astype(jnp.bfloat16)
        projected = jnp.dot(chosen, packed_ref[...], preferred_element_type=jnp.float32)
        gate = pre_ref[:, k, :units].astype(jnp.float32)
        up = pre_ref[:, k, units:].astype(jnp.float32)
        sigmoid = jax.nn.sigmoid(gate)
        silu = gate * sigmoid
        hidden = (silu * up).astype(jnp.bfloat16).astype(jnp.float32)
        sums.append(jnp.sum(projected * hidden, axis=1, keepdims=True))
        wide = (probs[:, k : k + 1] * projected).astype(jnp.bfloat16).astype(jnp.float32)
        grad_ref[:, k, :units] = (wide * up * sigmoid * (1.0 + gate * (1.0 - sigmoid))).astype(jnp.bfloat16)
        grad_ref[:, k, units:] = (wide * silu).astype(jnp.bfloat16)
    pair = lax.broadcasted_iota(jnp.int32, (tokens, LANES), 1)
    both = jnp.where(pair == 0, sums[0], jnp.where(pair == 1, sums[1], 0.0))
    grad_probs_ref[...] = both.T[:2, :].astype(jnp.bfloat16)


def add_kernel(count, kept_ref, *refs):
    out_ref, stage, sems = refs[count:]
    copies, at = [], 0
    for i, ref in enumerate(refs[:count]):
        rows = pl.ds(at, ref.shape[0])
        copies.append((rows, pltpu.make_async_copy(ref, stage.at[rows, :], sems.at[i])))
        copies[-1][1].start()
        at += ref.shape[0]
    for rows, copy in copies:
        copy.wait()
        out_ref[rows, :] = (kept_ref[rows, :] + stage[rows, :].astype(jnp.float32)).astype(jnp.bfloat16)


def local(grad_out, saved_pre, gate_probs, routes, down_weight):
    devices = lax.axis_size("expert")
    planes = lax.axis_size("dp")
    per_device, units, model_width = down_weight.shape
    tokens, per_token = routes.shape
    experts = per_device * devices
    capacity = 2 * tokens * per_token // experts
    me = lax.axis_index("expert").astype(jnp.int32)
    plane = lax.axis_index("dp").astype(jnp.int32)
    paired = planes == 4 and devices == 8
    width = model_width // 4
    used = per_token * units + LANES
    held = per_device * units
    everyone = devices * tokens

    if paired:
        near = plane ^ 1
        give, keep = 3 - plane, plane
        order = [give, 3 - near, keep, keep, 3 - near, near]
        order[1] = 3 - near
        sends = [give, 3 - near, near, keep, 3 - near, near]
    else:
        sends = [jnp.int32(i) for i in (0, 0, 0, 1, 2, 3)]
    plan = jnp.stack(sends).astype(jnp.int32)

    def staged(rows, columns):
        return pltpu.VMEM((rows, columns), jnp.bfloat16)

    lead, near_lead, rest, near_keep = call(
        functools.partial(lead_kernel, units, width),
        [
            shape(tokens, used + width),
            shape(tokens, used + width),
            shape(tokens, 3 * width),
            shape(tokens, width),
        ],
        [plan] + [in_hbm(v) for v in (saved_pre, gate_probs.T, routes.T, grad_out)],
        [SMEM] + [ANY] * 4,
        [
            pltpu.VMEM(saved_pre.shape, jnp.bfloat16),
            pltpu.VMEM((per_token, tokens), jnp.bfloat16),
            pltpu.VMEM((per_token, tokens), jnp.int32),
            pltpu.SemaphoreType.DMA((9,)),
        ],
    )

    def first(sources, plan, initial=(), cuts=(held,)):
        rows = sum(source.shape[0] for source in sources)
        kind = jnp.float32 if len(cuts) == 1 else jnp.bfloat16
        return call(
            functools.partial(first_kernel, units, per_device, tokens, len(sources), width, len(initial)),
            [shape(held, rows)] + [jax.ShapeDtypeStruct((cut, width), kind) for cut in cuts],
            [plan, *initial] + sources,
            [SMEM] + [VMEM] * len(initial) + [ANY] * len(sources),
            [staged(held, rows), staged(rows, used + width), pltpu.SemaphoreType.DMA((len(sources) + 1,))],
            mib=16,
            flops=2 * rows * held * width,
            out_specs=[pl.BlockSpec(memory_space=pltpu.HBM)] + [VMEM] * len(cuts),
        )

    def early(sources, plan, weight):
        rows = sum(source.shape[0] for source in sources)
        return call(
            functools.partial(early_kernel, units, per_device, tokens, len(sources), width, capacity),
            [
                jax.ShapeDtypeStruct((rows // tokens * per_device * capacity, units), jnp.float32),
                shape(rows // tokens * per_device * capacity, LANES),
            ],
            [plan, weight] + sources,
            [SMEM] + [ANY] * (1 + len(sources)),
            [
                staged(rows, LANES + width),
                staged(held, width),
                pltpu.VMEM((rows // tokens * per_device * capacity, width), jnp.float32),
                pltpu.SemaphoreType.DMA((len(sources) + 1,)),
            ],
            mib=16,
            flops=2 * rows * held * width,
        )

    def turn(plan):
        return call(
            functools.partial(turn_kernel, width),
            shape(3 * width, held),
            [plan, weight],
            [SMEM, ANY],
            [pltpu.VMEM((3, held, width), jnp.bfloat16), pltpu.SemaphoreType.DMA((3,))],
        )

    def project(total, chosen, turned, sources, plan):
        rows = sum(source.shape[0] for source in sources)
        return call(
            functools.partial(project_kernel, units, per_device, tokens, len(sources), width, capacity),
            shape(rows // tokens * per_device * capacity, units),
            [plan, total, chosen, turned] + sources,
            [SMEM] + [VMEM] * 3 + [ANY] * len(sources),
            [
                staged(rows, 3 * width),
                pltpu.VMEM((rows // tokens * per_device * capacity, 3 * width), jnp.float32),
                pltpu.SemaphoreType.DMA((len(sources),)),
            ],
            mib=24,
            flops=6 * rows * held * width,
        )

    def columns(hiddens, groups):
        sources = sum([list(group) for group, _ in groups], [])
        rows = sum(source.shape[0] for source in sources)
        return call(
            functools.partial(columns_kernel, [(len(group), at) for group, at in groups], width),
            jax.ShapeDtypeStruct((held, width), jnp.float32),
            hiddens + sources,
            [ANY] * (len(hiddens) + len(sources)),
            [
                staged(held, rows),
                staged(rows, width),
                pltpu.SemaphoreType.DMA((len(hiddens) + len(sources),)),
            ],
            mib=16,
            flops=2 * rows * held * width,
        )

    weight = in_hbm(down_weight.reshape(held, model_width))
    base = me * per_device
    if paired:
        plan = jnp.stack(
            [give, keep, 3 - near, near, base] + [me ^ offset for offset in block_offsets(me)]
        ).astype(jnp.int32)
        block = swap(near_lead, "dp", 4, 1)
        turned = turn(plan)
        own = gather_rows(lead, (), ((block, turned), (), ()))
        hidden, given = first(own, plan)
        hidden = in_hbm(hidden)
        block = after((block,), own[2], own[3])[0]
        sibling = swap(block, "expert", 8, 1)
        beside = send(block, "expert", STRAIGHT)
        second = send(after((sibling,), given)[0], "expert", STRAIGHT)
        corner = send(beside, "expert", CROSSWISE)
        soon = [block, sibling, beside, swap(after((beside,), given)[0], "expert", 8, 1)]
        soon_hidden, given = first(soon, plan, [given])
        soon_hidden = in_hbm(soon_hidden)
        total, chosen = early(own, plan, after((weight,), given)[0])
        second_over, corner_over = after((second, corner), given, total)
        later = [second, corner, swap(second_over, "expert", 8, 1), swap(corner_over, "expert", 8, 1)]
        later_hidden, *given = first(later, plan, [given], (3 * held // 16, held // 4, 9 * held // 16))
        crossed = [lax.ppermute(part, "dp", [(0, 3), (3, 0), (1, 2), (2, 1)]) for part in given]
        later_hidden = in_hbm(later_hidden)
        near_keep = lax.ppermute(after((near_keep,), own[4])[0], "dp", [(i, i ^ 1) for i in range(4)])
        rest = after((jnp.concatenate([rest, near_keep], 1),), later[2], later[3])[0]
        rests = gather_rows(in_hbm(rest), (crossed[0],), ((), (), (crossed[1],)), True, in_hbm)
        packed = in_vmem(project(total, chosen, turned, rests, plan))
        kept = columns(
            [hidden, soon_hidden, later_hidden],
            [
                (rests, 0),
                ([rests[i] for i in (0, 1, 2, 5)], 3 * width),
                ([rests[i] for i in (3, 4, 6, 7)], 3 * width),
            ],
        )
    else:
        own = lax.all_gather(lead, "expert", axis=0, tiled=True)
        rests = lax.all_gather(rest, "expert", axis=0, tiled=True)
        group = math.gcd(devices, 8)
        plan = jnp.concatenate(
            [jnp.arange(4, dtype=jnp.int32), base.reshape(1), jnp.arange(group, dtype=jnp.int32)]
        )
        partial, packs = 0.0, []
        for i in range(0, devices, group):
            rows = slice(i * tokens, (i + group) * tokens)
            hidden, given = first([own[rows]], plan)
            total, chosen = early([own[rows]], plan, weight)
            packs.append(project(total, chosen, turn(plan), [rests[rows]], plan))
            kept = [columns([hidden], [([rests[rows]], q * width)]) for q in range(3)]
            partial = partial + jnp.concatenate([given] + kept, 1)
        packed = jnp.concatenate(packs, 0)
        summed = lax.psum_scatter(partial.astype(jnp.bfloat16), "dp", scatter_dimension=1, tiled=True)

    returned = in_vmem(lax.all_to_all(packed, "expert", 0, 0, tiled=True))
    grad_pre, grad_probs = call(
        functools.partial(finish_kernel, units, capacity),
        [shape(tokens, per_token, 2 * units), shape(per_token, tokens)],
        [routes.T, saved_pre, gate_probs.T, returned],
        [VMEM] * 4,
    )
    if paired:
        crossed = [in_hbm(part) for part in crossed[:-1]] + list(after(crossed[-1:], grad_probs))
        summed = call(
            functools.partial(add_kernel, len(crossed)),
            shape(held, width),
            [kept] + crossed,
            [VMEM] + [ANY] * len(crossed),
            [staged(held, width), pltpu.SemaphoreType.DMA((len(crossed),))],
        )
    return grad_pre, grad_probs.T, summed.reshape(per_device, units, model_width // planes)


def solution(mesh):
    in_specs = (
        P(("dp", "expert"), None),
        P(("dp", "expert"), None, None),
        P(("dp", "expert"), None),
        P(("dp", "expert"), None),
        P("expert", None, None),
    )
    out_specs = (
        P(("dp", "expert"), None, None),
        P(("dp", "expert"), None),
        P("expert", None, "dp"),
    )
    return jax.shard_map(local, mesh=mesh, in_specs=in_specs, out_specs=out_specs, check_vma=False)
```

```python
import functools
import math

import jax
import jax.numpy as jnp
from jax import lax
from jax.experimental import pallas as pl
from jax.experimental.pallas import tpu as pltpu
from jax.sharding import PartitionSpec as P

LANES = 128
MIB = 1024 * 1024
ANY = pl.BlockSpec(memory_space=pl.ANY)
VMEM = pl.BlockSpec(memory_space=pltpu.VMEM)
SMEM = pl.BlockSpec(memory_space=pltpu.SMEM)


def call(kernel, outs, operands, specs, scratch=(), mib=12, flops=0, out_specs=None):
    arrays = list(operands) + (outs if isinstance(outs, list) else [outs])
    moved = sum(math.prod(v.shape) * jnp.dtype(v.dtype).itemsize for v in arrays)
    return pl.pallas_call(
        kernel,
        out_shape=outs,
        in_specs=specs,
        out_specs=out_specs or ([VMEM] * len(outs) if isinstance(outs, list) else VMEM),
        scratch_shapes=list(scratch),
        compiler_params=pltpu.CompilerParams(vmem_limit_bytes=mib * MIB),
        cost_estimate=pl.CostEstimate(flops=flops, transcendentals=0, bytes_accessed=moved),
    )(*operands)


def shape(*dims):
    return jax.ShapeDtypeStruct(dims, jnp.bfloat16)


def fetch(sources, first, width, stage, sems, start_row=0, start_sem=0):
    copies, at = [], start_row
    for i, source in enumerate(sources):
        rows = source.shape[0]
        copy = pltpu.make_async_copy(
            source.at[:, pl.ds(first, width)], stage.at[pl.ds(at, rows), :], sems.at[start_sem + i]
        )
        copy.start()
        copies.append(copy)
        at += rows
    return copies


def in_hbm(values):
    return pltpu.with_memory_space_constraint(values, pltpu.HBM)


def in_vmem(values):
    return pltpu.with_memory_space_constraint(values, pltpu.VMEM)


def send(values, axis, pairs, place=in_vmem):
    return place(lax.ppermute(values, axis, pairs))


def swap(values, axis, size, offset, place=in_vmem):
    return send(values, axis, [(i, i ^ offset) for i in range(size)], place)


STRAIGHT = [(i, i ^ (4 if i % 2 else 2)) for i in range(8)]
CROSSWISE = [(i, i ^ (2 if i % 2 else 4)) for i in range(8)]


def gather_rows(block, corner_hold=(), back=((), (), ()), in_turn=False, place=in_vmem):
    sibling = swap(block, "expert", 8, 1, place)
    first = send(block, "expert", STRAIGHT, place)
    second = send(sibling, "expert", STRAIGHT, place)
    hold = (*corner_hold, second) if in_turn else corner_hold
    corner = send(after((first,), *hold)[0], "expert", CROSSWISE, place)
    places = (place, in_vmem, in_vmem)
    over = [
        swap(after((v,), *holds)[0], "expert", 8, 1, last)
        for v, holds, last in zip((first, second, corner), back, places)
    ]
    return [block, sibling, first, second, corner] + over


def block_offsets(me):
    straight = jnp.where(me % 2 == 0, 2, 4).astype(jnp.int32)
    crosswise = 6 - straight
    return [0, 1, straight, straight + 1, 6, crosswise + 1, crosswise, 7]


def after(values, *others):
    return lax.optimization_barrier((*values, *others))[: len(values)] if others else values


def lead_kernel(units, width, plan_ref, *refs):
    pre_hbm, probs_hbm, names_hbm, grad_ref, own_ref, near_ref, rest_ref, keep_ref = refs[:8]
    pre_ref, probs_ref, names_ref, sems = refs[8:]
    tokens = own_ref.shape[0]
    used = 2 * units + LANES
    inputs = []
    for i, pair in enumerate(((names_hbm, names_ref), (probs_hbm, probs_ref), (pre_hbm, pre_ref))):
        inputs.append(pltpu.make_async_copy(*pair, sems.at[6 + i]))
        inputs[-1].start()
    targets = [
        own_ref.at[:, pl.ds(used, width)],
        near_ref.at[:, pl.ds(used, width)],
        keep_ref.at[:, pl.ds(0, width)],
    ] + [rest_ref.at[:, pl.ds(i * width, width)] for i in range(3)]
    copies = []
    for i, target in enumerate(targets):
        at = pl.multiple_of(plan_ref[i] * width, LANES)
        copies.append(pltpu.make_async_copy(grad_ref.at[:, pl.ds(at, width)], target, sems.at[i]))
        copies[-1].start()
    for copy in inputs:
        copy.wait()
    probs = probs_ref[...].astype(jnp.float32).T
    names = names_ref[...].astype(jnp.float32).T
    for k in range(2):
        gate = pre_ref[:, k, :units].astype(jnp.float32)
        up = pre_ref[:, k, units:].astype(jnp.float32)
        hidden = (gate * jax.nn.sigmoid(gate) * up).astype(jnp.bfloat16).astype(jnp.float32)
        scaled = (hidden * probs[:, k : k + 1]).astype(jnp.bfloat16)
        own_ref[:, k * units : (k + 1) * units] = scaled
        near_ref[:, k * units : (k + 1) * units] = scaled
    lane = lax.broadcasted_iota(jnp.int32, (tokens, LANES), 1)
    wide = jnp.where(lane == 0, names[:, 0:1], jnp.where(lane == 1, names[:, 1:2], 0.0)).astype(jnp.bfloat16)
    own_ref[:, 2 * units : used] = wide
    near_ref[:, 2 * units : used] = wide
    for copy in copies:
        copy.wait()


def masked(stage, out_ref, units, per_device, tokens, base):
    for d in range(stage.shape[0] // tokens):
        rows = pl.ds(d * tokens, tokens)
        names = stage[rows, 2 * units : 2 * units + LANES].astype(jnp.float32)
        values = [stage[rows, k * units : (k + 1) * units].astype(jnp.float32) for k in range(2)]
        for j in range(per_device):
            expert = (base + j).astype(jnp.float32)
            part = jnp.zeros((tokens, units), jnp.float32)
            for k in range(2):
                part = part + jnp.where(names[:, k : k + 1] == expert, values[k], 0.0)
            out_ref[j * units : (j + 1) * units, d * tokens : (d + 1) * tokens] = part.T.astype(jnp.bfloat16)


def times_weight(rows, weight):
    return lax.dot_general(rows, weight, (((1,), (1,)), ((), ())), preferred_element_type=jnp.float32)


def wait_all(copies):
    for copy in copies:
        copy.wait()


def turn_kernel(width, plan_ref, weight_hbm, out_ref, weight, sems):
    loads = []
    for q in range(3):
        at = pl.multiple_of(plan_ref[q + 1] * width, LANES)
        loads.append(pltpu.make_async_copy(weight_hbm.at[:, pl.ds(at, width)], weight.at[q], sems.at[q]))
        loads[-1].start()
    for q in range(3):
        loads[q].wait()
        out_ref[q * width : (q + 1) * width, :] = weight[q].T


def early_kernel(units, per_device, tokens, count, width, capacity, plan_ref, weight_hbm, *refs):
    sources = refs[:count]
    total_ref, chosen_ref, stage, weight, picked, sems = refs[count:]
    at = pl.multiple_of(plan_ref[0] * width, LANES)
    loaded = pltpu.make_async_copy(weight_hbm.at[:, pl.ds(at, width)], weight, sems.at[count])
    loaded.start()
    wait_all(fetch(sources, 2 * units, LANES + width, stage, sems))
    lane = lax.broadcasted_iota(jnp.int32, (tokens, LANES), 1)
    row = lax.broadcasted_iota(jnp.int32, (tokens, tokens), 0)
    col = lax.broadcasted_iota(jnp.int32, (tokens, tokens), 1)
    earlier = (row > col).astype(jnp.bfloat16)
    expert = (plan_ref[4] + lane // capacity).astype(jnp.float32)
    place = (lane % capacity).astype(jnp.float32)
    span = per_device * capacity
    usable = lane < span
    blocks = stage.shape[0] // tokens
    for d in range(blocks):
        rows = pl.ds(d * tokens, tokens)
        names = stage[rows, :LANES].astype(jnp.float32)
        named = ((names[:, 0:1] == expert) | (names[:, 1:2] == expert)) & usable
        rank = jnp.dot(earlier, named.astype(jnp.bfloat16), preferred_element_type=jnp.float32)
        chosen = jnp.where(named & (rank == place), 1.0, 0.0).T.astype(jnp.bfloat16)
        chosen_ref[d * span : (d + 1) * span, :] = chosen[:span, :]
        pick(chosen[:span, :], stage[rows, LANES:], picked, d, blocks, capacity)
    loaded.wait()
    for j in range(per_device):
        rows = pl.ds(j * blocks * capacity, blocks * capacity)
        total_ref[rows, :] = times_weight(picked[rows, :].astype(jnp.bfloat16), weight[j * units : (j + 1) * units, :])


def pick(chosen, values, picked, d, blocks, capacity):
    rows = jnp.dot(chosen, values, preferred_element_type=jnp.float32)
    for j in range(chosen.shape[0] // capacity):
        picked[pl.ds((j * blocks + d) * capacity, capacity), :] = rows[j * capacity : (j + 1) * capacity, :]


def first_kernel(units, per_device, tokens, count, width, started, plan_ref, *refs):
    sources = refs[started : started + count]
    hidden_hbm, *out_refs, hidden_ref, stage, sems = refs[started + count :]
    used = 2 * units + LANES
    wait_all(fetch(sources, 0, used + width, stage, sems))
    masked(stage, hidden_ref, units, per_device, tokens, plan_ref[4])
    stored = pltpu.make_async_copy(hidden_ref, hidden_hbm, sems.at[count])
    stored.start()
    part = jnp.dot(hidden_ref[...], stage[:, used:], preferred_element_type=jnp.float32)
    part = part + refs[0][...] if started else part
    at = 0
    for out_ref in out_refs:
        out_ref[...] = part[at : at + out_ref.shape[0], :].astype(out_ref.dtype)
        at += out_ref.shape[0]
    stored.wait()


def project_kernel(units, per_device, tokens, count, width, capacity, plan_ref, *refs):
    total_ref, chosen_ref, weight = refs[:3]
    sources = refs[3 : 3 + count]
    packed_ref, stage, picked, sems = refs[3 + count :]
    wait_all(fetch(sources, 0, 3 * width, stage, sems))
    span = per_device * capacity
    blocks = stage.shape[0] // tokens
    for d in range(blocks):
        pick(
            chosen_ref[d * span : (d + 1) * span, :],
            stage[pl.ds(d * tokens, tokens), :],
            picked,
            d,
            blocks,
            capacity,
        )
    projected = []
    for j in range(per_device):
        rows = pl.ds(j * blocks * capacity, blocks * capacity)
        part = jnp.dot(
            picked[rows, :].astype(jnp.bfloat16),
            weight[:, j * units : (j + 1) * units],
            preferred_element_type=jnp.float32,
        )
        projected.append(total_ref[rows, :] + part)
    for d in range(blocks):
        to = pl.multiple_of(plan_ref[5 + d] * span, 8)
        block = jnp.concatenate([values[d * capacity : (d + 1) * capacity, :] for values in projected], 0)
        packed_ref[pl.ds(to, span), :] = block.astype(jnp.bfloat16)


def columns_kernel(parts, width, *refs):
    at = len(parts)
    out_ref, hidden_ref, stage, sems = refs[-4:]
    waits, row, sem = [], 0, 0
    for i, (count, first) in enumerate(parts):
        sources = refs[at : at + count]
        rows = sum(source.shape[0] for source in sources)
        copies = fetch(sources, first, width, stage, sems, row, sem)
        copies.append(
            pltpu.make_async_copy(refs[i], hidden_ref.at[:, pl.ds(row, rows)], sems.at[sem + count])
        )
        copies[-1].start()
        waits.append((pl.ds(row, rows), copies))
        row += rows
        sem += count + 1
        at += count
    for i, (rows, copies) in enumerate(waits):
        wait_all(copies)
        part = jnp.dot(hidden_ref[:, rows], stage[rows, :], preferred_element_type=jnp.float32)
        out_ref[...] = part if i == 0 else out_ref[...] + part


def ready_kernel(units, capacity, names_ref, pre_ref, probs_ref, chosen_ref, hidden_ref, gate_ref, up_ref, wide_ref):
    tokens = names_ref.shape[1]
    slots = chosen_ref.shape[2]
    experts = slots // capacity
    e_lane = lax.broadcasted_iota(jnp.int32, (tokens, experts), 1).astype(jnp.float32)
    row = lax.broadcasted_iota(jnp.int32, (tokens, tokens), 0)
    col = lax.broadcasted_iota(jnp.int32, (tokens, tokens), 1)
    earlier = (row > col).astype(jnp.bfloat16)
    names = names_ref[...].astype(jnp.float32).T
    hits = [names[:, k : k + 1] == e_lane for k in range(2)]
    rank = jnp.dot(earlier, (hits[0] | hits[1]).astype(jnp.bfloat16), preferred_element_type=jnp.float32)
    lane = lax.broadcasted_iota(jnp.int32, (tokens, slots), 1).astype(jnp.float32)
    probs = probs_ref[...].astype(jnp.float32).T
    for k in range(2):
        mine = jnp.sum(jnp.where(hits[k], rank, 0.0), axis=1, keepdims=True)
        chosen_ref[k] = (lane == names[:, k : k + 1] * capacity + mine).astype(jnp.bfloat16)
        gate = pre_ref[:, k, :units].astype(jnp.float32)
        up = pre_ref[:, k, units:].astype(jnp.float32)
        sigmoid = jax.nn.sigmoid(gate)
        silu = gate * sigmoid
        hidden_ref[k] = (silu * up).astype(jnp.bfloat16)
        gate_ref[k] = up * sigmoid * (1.0 + gate * (1.0 - sigmoid))
        up_ref[k] = silu
        wide_ref[k] = jnp.broadcast_to(probs[:, k : k + 1], wide_ref.shape[1:])


def finish_kernel(units, chosen_ref, hidden_ref, gate_ref, up_ref, wide_ref, packed_ref, grad_ref, grad_probs_ref):
    tokens = grad_ref.shape[0]
    sums = []
    for k in range(2):
        projected = jnp.dot(chosen_ref[k], packed_ref[...], preferred_element_type=jnp.float32)
        sums.append(jnp.sum(projected * hidden_ref[k].astype(jnp.float32), axis=1, keepdims=True))
        wide = (wide_ref[k][:, :1] * projected).astype(jnp.bfloat16).astype(jnp.float32)
        grad_ref[:, k, :units] = (wide * gate_ref[k]).astype(jnp.bfloat16)
        grad_ref[:, k, units:] = (wide * up_ref[k]).astype(jnp.bfloat16)
    pair = lax.broadcasted_iota(jnp.int32, (tokens, LANES), 1)
    both = jnp.where(pair == 0, sums[0], jnp.where(pair == 1, sums[1], 0.0))
    grad_probs_ref[...] = both.T[:2, :].astype(jnp.bfloat16)


def add_kernel(count, kept_ref, *refs):
    out_ref, stage, sems = refs[count:]
    copies, at = [], 0
    for i, ref in enumerate(refs[:count]):
        rows = pl.ds(at, ref.shape[0])
        copies.append((rows, pltpu.make_async_copy(ref, stage.at[rows, :], sems.at[i])))
        copies[-1][1].start()
        at += ref.shape[0]
    for rows, copy in copies:
        copy.wait()
        out_ref[rows, :] = (kept_ref[rows, :] + stage[rows, :].astype(jnp.float32)).astype(jnp.bfloat16)


def local(grad_out, saved_pre, gate_probs, routes, down_weight):
    devices = lax.axis_size("expert")
    planes = lax.axis_size("dp")
    per_device, units, model_width = down_weight.shape
    tokens, per_token = routes.shape
    experts = per_device * devices
    capacity = 2 * tokens * per_token // experts
    me = lax.axis_index("expert").astype(jnp.int32)
    plane = lax.axis_index("dp").astype(jnp.int32)
    paired = planes == 4 and devices == 8
    width = model_width // 4
    used = per_token * units + LANES
    held = per_device * units
    everyone = devices * tokens

    if paired:
        near = plane ^ 1
        give, keep = 3 - plane, plane
        order = [give, 3 - near, keep, keep, 3 - near, near]
        order[1] = 3 - near
        sends = [give, 3 - near, near, keep, 3 - near, near]
    else:
        sends = [jnp.int32(i) for i in (0, 0, 0, 1, 2, 3)]
    plan = jnp.stack(sends).astype(jnp.int32)

    def staged(rows, columns):
        return pltpu.VMEM((rows, columns), jnp.bfloat16)

    lead, near_lead, rest, near_keep = call(
        functools.partial(lead_kernel, units, width),
        [
            shape(tokens, used + width),
            shape(tokens, used + width),
            shape(tokens, 3 * width),
            shape(tokens, width),
        ],
        [plan] + [in_hbm(v) for v in (saved_pre, gate_probs.T, routes.T, grad_out)],
        [SMEM] + [ANY] * 4,
        [
            pltpu.VMEM(saved_pre.shape, jnp.bfloat16),
            pltpu.VMEM((per_token, tokens), jnp.bfloat16),
            pltpu.VMEM((per_token, tokens), jnp.int32),
            pltpu.SemaphoreType.DMA((9,)),
        ],
    )

    def first(sources, plan, initial=(), cuts=(held,)):
        rows = sum(source.shape[0] for source in sources)
        kind = jnp.float32 if len(cuts) == 1 else jnp.bfloat16
        return call(
            functools.partial(first_kernel, units, per_device, tokens, len(sources), width, len(initial)),
            [shape(held, rows)] + [jax.ShapeDtypeStruct((cut, width), kind) for cut in cuts],
            [plan, *initial] + sources,
            [SMEM] + [VMEM] * len(initial) + [ANY] * len(sources),
            [staged(held, rows), staged(rows, used + width), pltpu.SemaphoreType.DMA((len(sources) + 1,))],
            mib=16,
            flops=2 * rows * held * width,
            out_specs=[pl.BlockSpec(memory_space=pltpu.HBM)] + [VMEM] * len(cuts),
        )

    def early(sources, plan, weight):
        rows = sum(source.shape[0] for source in sources)
        return call(
            functools.partial(early_kernel, units, per_device, tokens, len(sources), width, capacity),
            [
                jax.ShapeDtypeStruct((rows // tokens * per_device * capacity, units), jnp.float32),
                shape(rows // tokens * per_device * capacity, LANES),
            ],
            [plan, weight] + sources,
            [SMEM] + [ANY] * (1 + len(sources)),
            [
                staged(rows, LANES + width),
                staged(held, width),
                pltpu.VMEM((rows // tokens * per_device * capacity, width), jnp.float32),
                pltpu.SemaphoreType.DMA((len(sources) + 1,)),
            ],
            mib=16,
            flops=2 * rows * held * width,
        )

    def turn(plan, weight):
        return call(
            functools.partial(turn_kernel, width),
            shape(3 * width, held),
            [plan, weight],
            [SMEM, ANY],
            [pltpu.VMEM((3, held, width), jnp.bfloat16), pltpu.SemaphoreType.DMA((3,))],
        )

    def project(total, chosen, turned, sources, plan):
        rows = sum(source.shape[0] for source in sources)
        return call(
            functools.partial(project_kernel, units, per_device, tokens, len(sources), width, capacity),
            shape(rows // tokens * per_device * capacity, units),
            [plan, total, chosen, turned] + sources,
            [SMEM] + [VMEM] * 3 + [ANY] * len(sources),
            [
                staged(rows, 3 * width),
                pltpu.VMEM((rows // tokens * per_device * capacity, 3 * width), jnp.float32),
                pltpu.SemaphoreType.DMA((len(sources),)),
            ],
            mib=24,
            flops=6 * rows * held * width,
        )

    def columns(hiddens, groups):
        sources = sum([list(group) for group, _ in groups], [])
        rows = sum(source.shape[0] for source in sources)
        return call(
            functools.partial(columns_kernel, [(len(group), at) for group, at in groups], width),
            jax.ShapeDtypeStruct((held, width), jnp.float32),
            hiddens + sources,
            [ANY] * (len(hiddens) + len(sources)),
            [
                staged(held, rows),
                staged(rows, width),
                pltpu.SemaphoreType.DMA((len(hiddens) + len(sources),)),
            ],
            mib=16,
            flops=2 * rows * held * width,
        )

    weight = in_hbm(down_weight.reshape(held, model_width))
    base = me * per_device
    if paired:
        plan = jnp.stack(
            [give, keep, 3 - near, near, base] + [me ^ offset for offset in block_offsets(me)]
        ).astype(jnp.int32)
        block = swap(near_lead, "dp", 4, 1)
        own = gather_rows(lead, (), ((block,), (), ()))
        hidden, given = first(own, plan)
        hidden = in_hbm(hidden)
        near_rows = gather_rows(after((block,), own[2], own[3])[0], (), ((given,), (given,), (given,)))
        near_hidden, *given = first(near_rows, plan, [given], (3 * held // 16, held // 4, 9 * held // 16))
        crossed = [lax.ppermute(part, "dp", [(0, 3), (3, 0), (1, 2), (2, 1)]) for part in given]
        near_hidden = in_hbm(near_hidden)
        near_keep = lax.ppermute(after((near_keep,), own[4])[0], "dp", [(i, i ^ 1) for i in range(4)])
        rest = after((jnp.concatenate([rest, near_keep], 1),), near_rows[6], near_rows[7])[0]
        total, chosen = early([in_hbm(v) for v in own], plan, after((weight,), crossed[0])[0])
        turned = turn(plan, after((weight,), given[0])[0])
        rests = gather_rows(in_hbm(rest), (crossed[0], turned), ((), (), (crossed[1], total)), True, in_hbm)
        packed = in_vmem(project(total, chosen, turned, rests, plan))
        late = [in_hbm(v) for v in after(tuple(rests[6:]), packed)]
        kept = columns([hidden, near_hidden], [(rests[:6] + late, 0), (rests[:6] + late, 3 * width)])
    else:
        own = lax.all_gather(lead, "expert", axis=0, tiled=True)
        rests = lax.all_gather(rest, "expert", axis=0, tiled=True)
        group = math.gcd(devices, 8)
        plan = jnp.concatenate(
            [jnp.arange(4, dtype=jnp.int32), base.reshape(1), jnp.arange(group, dtype=jnp.int32)]
        )
        partial, packs = 0.0, []
        for i in range(0, devices, group):
            rows = slice(i * tokens, (i + group) * tokens)
            hidden, given = first([own[rows]], plan)
            total, chosen = early([own[rows]], plan, weight)
            packs.append(project(total, chosen, turn(plan, weight), [rests[rows]], plan))
            kept = [columns([hidden], [([rests[rows]], q * width)]) for q in range(3)]
            partial = partial + jnp.concatenate([given] + kept, 1)
        packed = jnp.concatenate(packs, 0)
        summed = lax.psum_scatter(partial.astype(jnp.bfloat16), "dp", scatter_dimension=1, tiled=True)

    returned = in_vmem(lax.all_to_all(packed, "expert", 0, 0, tiled=True))
    slots = devices * per_device * capacity
    ready = call(
        functools.partial(ready_kernel, units, capacity),
        [
            shape(per_token, tokens, slots),
            shape(per_token, tokens, units),
            jax.ShapeDtypeStruct((per_token, tokens, units), jnp.float32),
            jax.ShapeDtypeStruct((per_token, tokens, units), jnp.float32),
            jax.ShapeDtypeStruct((per_token, tokens, LANES), jnp.float32),
        ],
        [after((routes.T,), kept if paired else packed)[0], saved_pre, gate_probs.T],
        [VMEM] * 3,
    )
    grad_pre, grad_probs = call(
        functools.partial(finish_kernel, units),
        [shape(tokens, per_token, 2 * units), shape(per_token, tokens)],
        [in_vmem(values) for values in ready] + [returned],
        [VMEM] * 6,
    )
    if paired:
        crossed = [in_hbm(part) for part in crossed[:-1]] + list(after(crossed[-1:], grad_probs))
        summed = call(
            functools.partial(add_kernel, len(crossed)),
            shape(held, width),
            [kept] + crossed,
            [VMEM] + [ANY] * len(crossed),
            [staged(held, width), pltpu.SemaphoreType.DMA((len(crossed),))],
        )
    return grad_pre, grad_probs.T, summed.reshape(per_device, units, model_width // planes)


def solution(mesh):
    in_specs = (
        P(("dp", "expert"), None),
        P(("dp", "expert"), None, None),
        P(("dp", "expert"), None),
        P(("dp", "expert"), None),
        P("expert", None, None),
    )
    out_specs = (
        P(("dp", "expert"), None, None),
        P(("dp", "expert"), None),
        P("expert", None, "dp"),
    )
    return jax.shard_map(local, mesh=mesh, in_specs=in_specs, out_specs=out_specs, check_vma=False)
```

```python
import functools
import math

import jax
import jax.numpy as jnp
from jax import lax
from jax.experimental import pallas as pl
from jax.experimental.pallas import tpu as pltpu
from jax.sharding import PartitionSpec as P

LANES = 128
MIB = 1024 * 1024
ANY = pl.BlockSpec(memory_space=pl.ANY)
VMEM = pl.BlockSpec(memory_space=pltpu.VMEM)
SMEM = pl.BlockSpec(memory_space=pltpu.SMEM)


def call(kernel, outs, operands, specs, scratch=(), mib=12, flops=0, out_specs=None):
    arrays = list(operands) + (outs if isinstance(outs, list) else [outs])
    moved = sum(math.prod(v.shape) * jnp.dtype(v.dtype).itemsize for v in arrays)
    return pl.pallas_call(
        kernel,
        out_shape=outs,
        in_specs=specs,
        out_specs=out_specs or ([VMEM] * len(outs) if isinstance(outs, list) else VMEM),
        scratch_shapes=list(scratch),
        compiler_params=pltpu.CompilerParams(vmem_limit_bytes=mib * MIB),
        cost_estimate=pl.CostEstimate(flops=flops, transcendentals=0, bytes_accessed=moved),
    )(*operands)


def shape(*dims):
    return jax.ShapeDtypeStruct(dims, jnp.bfloat16)


def fetch(sources, first, width, stage, sems, start_row=0, start_sem=0):
    copies, at = [], start_row
    for i, source in enumerate(sources):
        rows = source.shape[0]
        copy = pltpu.make_async_copy(
            source.at[:, pl.ds(first, width)], stage.at[pl.ds(at, rows), :], sems.at[start_sem + i]
        )
        copy.start()
        copies.append(copy)
        at += rows
    return copies


def in_hbm(values):
    return pltpu.with_memory_space_constraint(values, pltpu.HBM)


def in_vmem(values):
    return pltpu.with_memory_space_constraint(values, pltpu.VMEM)


def send(values, axis, pairs, place=in_vmem):
    return place(lax.ppermute(values, axis, pairs))


def swap(values, axis, size, offset, place=in_vmem):
    return send(values, axis, [(i, i ^ offset) for i in range(size)], place)


STRAIGHT = [(i, i ^ (4 if i % 2 else 2)) for i in range(8)]
CROSSWISE = [(i, i ^ (2 if i % 2 else 4)) for i in range(8)]


def gather_rows(block, corner_hold=(), back=((), (), ()), in_turn=False, place=in_vmem):
    sibling = swap(block, "expert", 8, 1, place)
    first = send(block, "expert", STRAIGHT, place)
    second = send(sibling, "expert", STRAIGHT, place)
    hold = (*corner_hold, second) if in_turn else corner_hold
    corner = send(after((first,), *hold)[0], "expert", CROSSWISE, place)
    places = (in_vmem, in_vmem, in_vmem)
    over = [
        swap(after((v,), *holds)[0], "expert", 8, 1, last)
        for v, holds, last in zip((first, second, corner), back, places)
    ]
    return [block, sibling, first, second, corner] + over


def block_offsets(me):
    straight = jnp.where(me % 2 == 0, 2, 4).astype(jnp.int32)
    crosswise = 6 - straight
    return [0, 1, straight, straight + 1, 6, crosswise + 1, crosswise, 7]


def after(values, *others):
    return lax.optimization_barrier((*values, *others))[: len(values)] if others else values


def lead_kernel(units, width, plan_ref, *refs):
    pre_hbm, probs_hbm, names_hbm, grad_ref, own_ref, near_ref, rest_ref, keep_ref = refs[:8]
    pre_ref, probs_ref, names_ref, sems = refs[8:]
    tokens = own_ref.shape[0]
    used = 2 * units + LANES
    inputs = []
    for i, pair in enumerate(((names_hbm, names_ref), (probs_hbm, probs_ref), (pre_hbm, pre_ref))):
        inputs.append(pltpu.make_async_copy(*pair, sems.at[6 + i]))
        inputs[-1].start()
    targets = [
        own_ref.at[:, pl.ds(used, width)],
        near_ref.at[:, pl.ds(used, width)],
        keep_ref.at[:, pl.ds(0, width)],
    ] + [rest_ref.at[:, pl.ds(i * width, width)] for i in range(3)]
    copies = []
    for i, target in enumerate(targets):
        at = pl.multiple_of(plan_ref[i] * width, LANES)
        copies.append(pltpu.make_async_copy(grad_ref.at[:, pl.ds(at, width)], target, sems.at[i]))
        copies[-1].start()
    for copy in inputs:
        copy.wait()
    probs = probs_ref[...].astype(jnp.float32).T
    names = names_ref[...].astype(jnp.float32).T
    for k in range(2):
        gate = pre_ref[:, k, :units].astype(jnp.float32)
        up = pre_ref[:, k, units:].astype(jnp.float32)
        hidden = (gate * jax.nn.sigmoid(gate) * up).astype(jnp.bfloat16).astype(jnp.float32)
        scaled = (hidden * probs[:, k : k + 1]).astype(jnp.bfloat16)
        own_ref[:, k * units : (k + 1) * units] = scaled
        near_ref[:, k * units : (k + 1) * units] = scaled
    lane = lax.broadcasted_iota(jnp.int32, (tokens, LANES), 1)
    wide = jnp.where(lane == 0, names[:, 0:1], jnp.where(lane == 1, names[:, 1:2], 0.0)).astype(jnp.bfloat16)
    own_ref[:, 2 * units : used] = wide
    near_ref[:, 2 * units : used] = wide
    for copy in copies:
        copy.wait()


def masked(stage, out_ref, units, per_device, tokens, base):
    for d in range(stage.shape[0] // tokens):
        rows = pl.ds(d * tokens, tokens)
        names = stage[rows, 2 * units : 2 * units + LANES].astype(jnp.float32)
        values = [stage[rows, k * units : (k + 1) * units].astype(jnp.float32) for k in range(2)]
        for j in range(per_device):
            expert = (base + j).astype(jnp.float32)
            part = jnp.zeros((tokens, units), jnp.float32)
            for k in range(2):
                part = part + jnp.where(names[:, k : k + 1] == expert, values[k], 0.0)
            out_ref[j * units : (j + 1) * units, d * tokens : (d + 1) * tokens] = part.T.astype(jnp.bfloat16)


def times_weight(rows, weight):
    return lax.dot_general(rows, weight, (((1,), (1,)), ((), ())), preferred_element_type=jnp.float32)


def wait_all(copies):
    for copy in copies:
        copy.wait()


def turn_kernel(width, plan_ref, weight_hbm, out_ref, weight, sems):
    loads = []
    for q in range(3):
        at = pl.multiple_of(plan_ref[q + 1] * width, LANES)
        loads.append(pltpu.make_async_copy(weight_hbm.at[:, pl.ds(at, width)], weight.at[q], sems.at[q]))
        loads[-1].start()
    for q in range(3):
        loads[q].wait()
        out_ref[q * width : (q + 1) * width, :] = weight[q].T


def early_kernel(units, per_device, tokens, count, width, capacity, plan_ref, weight_hbm, *refs):
    sources = refs[:count]
    total_ref, chosen_ref, stage, weight, picked, sems = refs[count:]
    at = pl.multiple_of(plan_ref[0] * width, LANES)
    loaded = pltpu.make_async_copy(weight_hbm.at[:, pl.ds(at, width)], weight, sems.at[count])
    loaded.start()
    wait_all(fetch(sources, 2 * units, LANES + width, stage, sems))
    lane = lax.broadcasted_iota(jnp.int32, (tokens, LANES), 1)
    row = lax.broadcasted_iota(jnp.int32, (tokens, tokens), 0)
    col = lax.broadcasted_iota(jnp.int32, (tokens, tokens), 1)
    earlier = (row > col).astype(jnp.bfloat16)
    expert = (plan_ref[4] + lane // capacity).astype(jnp.float32)
    place = (lane % capacity).astype(jnp.float32)
    span = per_device * capacity
    usable = lane < span
    blocks = stage.shape[0] // tokens
    for d in range(blocks):
        rows = pl.ds(d * tokens, tokens)
        names = stage[rows, :LANES].astype(jnp.float32)
        named = ((names[:, 0:1] == expert) | (names[:, 1:2] == expert)) & usable
        rank = jnp.dot(earlier, named.astype(jnp.bfloat16), preferred_element_type=jnp.float32)
        chosen = jnp.where(named & (rank == place), 1.0, 0.0).T.astype(jnp.bfloat16)
        chosen_ref[d * span : (d + 1) * span, :] = chosen[:span, :]
        pick(chosen[:span, :], stage[rows, LANES:], picked, d, blocks, capacity)
    loaded.wait()
    for j in range(per_device):
        rows = pl.ds(j * blocks * capacity, blocks * capacity)
        total_ref[rows, :] = times_weight(picked[rows, :].astype(jnp.bfloat16), weight[j * units : (j + 1) * units, :])


def pick(chosen, values, picked, d, blocks, capacity):
    rows = jnp.dot(chosen, values, preferred_element_type=jnp.float32)
    for j in range(chosen.shape[0] // capacity):
        picked[pl.ds((j * blocks + d) * capacity, capacity), :] = rows[j * capacity : (j + 1) * capacity, :]


def first_kernel(units, per_device, tokens, count, width, started, plan_ref, *refs):
    sources = refs[started : started + count]
    hidden_hbm, *out_refs, hidden_ref, stage, sems = refs[started + count :]
    used = 2 * units + LANES
    wait_all(fetch(sources, 0, used + width, stage, sems))
    masked(stage, hidden_ref, units, per_device, tokens, plan_ref[4])
    stored = pltpu.make_async_copy(hidden_ref, hidden_hbm, sems.at[count])
    stored.start()
    part = jnp.dot(hidden_ref[...], stage[:, used:], preferred_element_type=jnp.float32)
    part = part + refs[0][...] if started else part
    at = 0
    for out_ref in out_refs:
        out_ref[...] = part[at : at + out_ref.shape[0], :].astype(out_ref.dtype)
        at += out_ref.shape[0]
    stored.wait()


def project_kernel(units, per_device, tokens, count, width, capacity, plan_ref, *refs):
    total_ref, chosen_ref, weight = refs[:3]
    sources = refs[3 : 3 + count]
    packed_ref, stage, picked, sems = refs[3 + count :]
    wait_all(fetch(sources, 0, 3 * width, stage, sems))
    span = per_device * capacity
    blocks = stage.shape[0] // tokens
    for d in range(blocks):
        pick(
            chosen_ref[d * span : (d + 1) * span, :],
            stage[pl.ds(d * tokens, tokens), :],
            picked,
            d,
            blocks,
            capacity,
        )
    projected = []
    for j in range(per_device):
        rows = pl.ds(j * blocks * capacity, blocks * capacity)
        part = jnp.dot(
            picked[rows, :].astype(jnp.bfloat16),
            weight[:, j * units : (j + 1) * units],
            preferred_element_type=jnp.float32,
        )
        projected.append(total_ref[rows, :] + part)
    for d in range(blocks):
        to = pl.multiple_of(plan_ref[5 + d] * span, 8)
        block = jnp.concatenate([values[d * capacity : (d + 1) * capacity, :] for values in projected], 0)
        packed_ref[pl.ds(to, span), :] = block.astype(jnp.bfloat16)


def columns_kernel(parts, width, *refs):
    at = len(parts)
    out_ref, hidden_ref, stage, sems = refs[-4:]
    waits, row, sem = [], 0, 0
    for i, (count, first) in enumerate(parts):
        sources = refs[at : at + count]
        rows = sum(source.shape[0] for source in sources)
        copies = fetch(sources, first, width, stage, sems, row, sem)
        copies.append(
            pltpu.make_async_copy(refs[i], hidden_ref.at[:, pl.ds(row, rows)], sems.at[sem + count])
        )
        copies[-1].start()
        waits.append((pl.ds(row, rows), copies))
        row += rows
        sem += count + 1
        at += count
    for i, (rows, copies) in enumerate(waits):
        wait_all(copies)
        part = jnp.dot(hidden_ref[:, rows], stage[rows, :], preferred_element_type=jnp.float32)
        out_ref[...] = part if i == 0 else out_ref[...] + part


def ready_kernel(units, capacity, names_ref, pre_ref, probs_ref, chosen_ref, hidden_ref, factor_ref, wide_ref):
    tokens = names_ref.shape[1]
    slots = chosen_ref.shape[2]
    experts = slots // capacity
    e_lane = lax.broadcasted_iota(jnp.int32, (tokens, experts), 1).astype(jnp.float32)
    row = lax.broadcasted_iota(jnp.int32, (tokens, tokens), 0)
    col = lax.broadcasted_iota(jnp.int32, (tokens, tokens), 1)
    earlier = (row > col).astype(jnp.bfloat16)
    names = names_ref[...].astype(jnp.float32).T
    hits = [names[:, k : k + 1] == e_lane for k in range(2)]
    rank = jnp.dot(earlier, (hits[0] | hits[1]).astype(jnp.bfloat16), preferred_element_type=jnp.float32)
    lane = lax.broadcasted_iota(jnp.int32, (tokens, slots), 1).astype(jnp.float32)
    probs = probs_ref[...].astype(jnp.float32).T
    for k in range(2):
        mine = jnp.sum(jnp.where(hits[k], rank, 0.0), axis=1, keepdims=True)
        chosen_ref[k] = (lane == names[:, k : k + 1] * capacity + mine).astype(jnp.bfloat16)
        gate = pre_ref[:, k, :units].astype(jnp.float32)
        up = pre_ref[:, k, units:].astype(jnp.float32)
        sigmoid = jax.nn.sigmoid(gate)
        silu = gate * sigmoid
        hidden_ref[k] = (silu * up).astype(jnp.bfloat16)
        factor_ref[k, :, :units] = up * sigmoid * (1.0 + gate * (1.0 - sigmoid))
        factor_ref[k, :, units:] = silu
        wide_ref[k] = jnp.broadcast_to(probs[:, k : k + 1], wide_ref.shape[1:])


def finish_kernel(units, chosen_ref, hidden_ref, factor_ref, wide_ref, packed_ref, grad_ref, grad_probs_ref):
    tokens = grad_ref.shape[0]
    sums = []
    for k in range(2):
        projected = jnp.dot(chosen_ref[k], packed_ref[...], preferred_element_type=jnp.float32)
        sums.append(jnp.sum(projected * hidden_ref[k].astype(jnp.float32), axis=1, keepdims=True))
        wide = (wide_ref[k][:, :1] * projected).astype(jnp.bfloat16).astype(jnp.float32)
        grad_ref[:, k, :units] = (wide * factor_ref[k, :, :units]).astype(jnp.bfloat16)
        grad_ref[:, k, units:] = (wide * factor_ref[k, :, units:]).astype(jnp.bfloat16)
    pair = lax.broadcasted_iota(jnp.int32, (tokens, LANES), 1)
    both = jnp.where(pair == 0, sums[0], jnp.where(pair == 1, sums[1], 0.0))
    grad_probs_ref[...] = both.T[:2, :].astype(jnp.bfloat16)


def add_kernel(count, kept_ref, *refs):
    out_ref, stage, sems = refs[count:]
    copies, at = [], 0
    for i, ref in enumerate(refs[:count]):
        rows = pl.ds(at, ref.shape[0])
        copies.append((rows, pltpu.make_async_copy(ref, stage.at[rows, :], sems.at[i])))
        copies[-1][1].start()
        at += ref.shape[0]
    for rows, copy in copies:
        copy.wait()
        out_ref[rows, :] = (kept_ref[rows, :] + stage[rows, :].astype(jnp.float32)).astype(jnp.bfloat16)


def local(grad_out, saved_pre, gate_probs, routes, down_weight):
    devices = lax.axis_size("expert")
    planes = lax.axis_size("dp")
    per_device, units, model_width = down_weight.shape
    tokens, per_token = routes.shape
    experts = per_device * devices
    capacity = 2 * tokens * per_token // experts
    me = lax.axis_index("expert").astype(jnp.int32)
    plane = lax.axis_index("dp").astype(jnp.int32)
    paired = planes == 4 and devices == 8
    width = model_width // 4
    used = per_token * units + LANES
    held = per_device * units
    everyone = devices * tokens

    if paired:
        near = plane ^ 1
        give, keep = 3 - plane, plane
        order = [give, 3 - near, keep, keep, 3 - near, near]
        order[1] = 3 - near
        sends = [give, 3 - near, near, keep, 3 - near, near]
    else:
        sends = [jnp.int32(i) for i in (0, 0, 0, 1, 2, 3)]
    plan = jnp.stack(sends).astype(jnp.int32)

    def staged(rows, columns):
        return pltpu.VMEM((rows, columns), jnp.bfloat16)

    lead, near_lead, rest, near_keep = call(
        functools.partial(lead_kernel, units, width),
        [
            shape(tokens, used + width),
            shape(tokens, used + width),
            shape(tokens, 3 * width),
            shape(tokens, width),
        ],
        [plan] + [in_hbm(v) for v in (saved_pre, gate_probs.T, routes.T, grad_out)],
        [SMEM] + [ANY] * 4,
        [
            pltpu.VMEM(saved_pre.shape, jnp.bfloat16),
            pltpu.VMEM((per_token, tokens), jnp.bfloat16),
            pltpu.VMEM((per_token, tokens), jnp.int32),
            pltpu.SemaphoreType.DMA((9,)),
        ],
    )

    def first(sources, plan, initial=(), cuts=(held,)):
        rows = sum(source.shape[0] for source in sources)
        kind = jnp.float32 if len(cuts) == 1 else jnp.bfloat16
        return call(
            functools.partial(first_kernel, units, per_device, tokens, len(sources), width, len(initial)),
            [shape(held, rows)] + [jax.ShapeDtypeStruct((cut, width), kind) for cut in cuts],
            [plan, *initial] + sources,
            [SMEM] + [VMEM] * len(initial) + [ANY] * len(sources),
            [staged(held, rows), staged(rows, used + width), pltpu.SemaphoreType.DMA((len(sources) + 1,))],
            mib=16,
            flops=2 * rows * held * width,
            out_specs=[pl.BlockSpec(memory_space=pltpu.HBM)] + [VMEM] * len(cuts),
        )

    def early(sources, plan, weight):
        rows = sum(source.shape[0] for source in sources)
        return call(
            functools.partial(early_kernel, units, per_device, tokens, len(sources), width, capacity),
            [
                jax.ShapeDtypeStruct((rows // tokens * per_device * capacity, units), jnp.float32),
                shape(rows // tokens * per_device * capacity, LANES),
            ],
            [plan, weight] + sources,
            [SMEM] + [ANY] * (1 + len(sources)),
            [
                staged(rows, LANES + width),
                staged(held, width),
                pltpu.VMEM((rows // tokens * per_device * capacity, width), jnp.float32),
                pltpu.SemaphoreType.DMA((len(sources) + 1,)),
            ],
            mib=16,
            flops=2 * rows * held * width,
        )

    def turn(plan, weight):
        return call(
            functools.partial(turn_kernel, width),
            shape(3 * width, held),
            [plan, weight],
            [SMEM, ANY],
            [pltpu.VMEM((3, held, width), jnp.bfloat16), pltpu.SemaphoreType.DMA((3,))],
        )

    def project(total, chosen, turned, sources, plan):
        rows = sum(source.shape[0] for source in sources)
        return call(
            functools.partial(project_kernel, units, per_device, tokens, len(sources), width, capacity),
            shape(rows // tokens * per_device * capacity, units),
            [plan, total, chosen, turned] + sources,
            [SMEM] + [VMEM] * 3 + [ANY] * len(sources),
            [
                staged(rows, 3 * width),
                pltpu.VMEM((rows // tokens * per_device * capacity, 3 * width), jnp.float32),
                pltpu.SemaphoreType.DMA((len(sources),)),
            ],
            mib=24,
            flops=6 * rows * held * width,
        )

    def columns(hiddens, groups):
        sources = sum([list(group) for group, _ in groups], [])
        rows = sum(source.shape[0] for source in sources)
        return call(
            functools.partial(columns_kernel, [(len(group), at) for group, at in groups], width),
            jax.ShapeDtypeStruct((held, width), jnp.float32),
            hiddens + sources,
            [ANY] * (len(hiddens) + len(sources)),
            [
                staged(held, rows),
                staged(rows, width),
                pltpu.SemaphoreType.DMA((len(hiddens) + len(sources),)),
            ],
            mib=16,
            flops=2 * rows * held * width,
        )

    weight = in_hbm(down_weight.reshape(held, model_width))
    base = me * per_device
    if paired:
        plan = jnp.stack(
            [give, keep, 3 - near, near, base] + [me ^ offset for offset in block_offsets(me)]
        ).astype(jnp.int32)
        block = swap(near_lead, "dp", 4, 1)
        own = gather_rows(lead, (), ((block,), (), ()))
        hidden, given = first(own, plan)
        hidden = in_hbm(hidden)
        near_rows = gather_rows(after((block,), own[2], own[3])[0], (), ((given,), (given,), (given,)))
        near_hidden, *given = first(near_rows, plan, [given], (3 * held // 16, held // 4, 9 * held // 16))
        crossed = [lax.ppermute(part, "dp", [(0, 3), (3, 0), (1, 2), (2, 1)]) for part in given]
        near_hidden = in_hbm(near_hidden)
        near_keep = lax.ppermute(after((near_keep,), own[4])[0], "dp", [(i, i ^ 1) for i in range(4)])
        rest = after((jnp.concatenate([rest, near_keep], 1),), near_rows[6], near_rows[7])[0]
        total, chosen = early([in_hbm(v) for v in own], plan, after((weight,), crossed[0])[0])
        turned = turn(plan, after((weight,), given[0])[0])
        rests = gather_rows(in_hbm(rest), (crossed[0], turned), ((), (), (crossed[1], total)), True, in_hbm)
        packed = in_vmem(project(total, chosen, turned, rests, plan))
        late = [in_hbm(v) for v in after(tuple(rests[5:]), packed)]
        kept = columns([hidden, near_hidden], [(rests[:5] + late, 0), (rests[:5] + late, 3 * width)])
    else:
        own = lax.all_gather(lead, "expert", axis=0, tiled=True)
        rests = lax.all_gather(rest, "expert", axis=0, tiled=True)
        group = math.gcd(devices, 8)
        plan = jnp.concatenate(
            [jnp.arange(4, dtype=jnp.int32), base.reshape(1), jnp.arange(group, dtype=jnp.int32)]
        )
        partial, packs = 0.0, []
        for i in range(0, devices, group):
            rows = slice(i * tokens, (i + group) * tokens)
            hidden, given = first([own[rows]], plan)
            total, chosen = early([own[rows]], plan, weight)
            packs.append(project(total, chosen, turn(plan, weight), [rests[rows]], plan))
            kept = [columns([hidden], [([rests[rows]], q * width)]) for q in range(3)]
            partial = partial + jnp.concatenate([given] + kept, 1)
        packed = jnp.concatenate(packs, 0)
        summed = lax.psum_scatter(partial.astype(jnp.bfloat16), "dp", scatter_dimension=1, tiled=True)

    returned = in_vmem(lax.all_to_all(packed, "expert", 0, 0, tiled=True))
    slots = devices * per_device * capacity
    ready = call(
        functools.partial(ready_kernel, units, capacity),
        [
            shape(per_token, tokens, slots),
            shape(per_token, tokens, units),
            jax.ShapeDtypeStruct((per_token, tokens, 2 * units), jnp.float32),
            jax.ShapeDtypeStruct((per_token, tokens, LANES), jnp.float32),
        ],
        [after((routes.T,), kept if paired else packed)[0], saved_pre, gate_probs.T],
        [VMEM] * 3,
    )
    grad_pre, grad_probs = call(
        functools.partial(finish_kernel, units),
        [shape(tokens, per_token, 2 * units), shape(per_token, tokens)],
        [in_vmem(values) for values in ready] + [returned],
        [VMEM] * 5,
    )
    if paired:
        settled = [in_hbm(crossed[0]), in_hbm(after((crossed[1],), packed)[0])]
        crossed = settled + list(after(crossed[-1:], grad_probs))
        summed = call(
            functools.partial(add_kernel, len(crossed)),
            shape(held, width),
            [kept] + crossed,
            [VMEM] + [ANY] * len(crossed),
            [staged(held, width), pltpu.SemaphoreType.DMA((len(crossed),))],
        )
    return grad_pre, grad_probs.T, summed.reshape(per_device, units, model_width // planes)


def solution(mesh):
    in_specs = (
        P(("dp", "expert"), None),
        P(("dp", "expert"), None, None),
        P(("dp", "expert"), None),
        P(("dp", "expert"), None),
        P("expert", None, None),
    )
    out_specs = (
        P(("dp", "expert"), None, None),
        P(("dp", "expert"), None),
        P("expert", None, "dp"),
    )
    return jax.shard_map(local, mesh=mesh, in_specs=in_specs, out_specs=out_specs, check_vma=False)
```

```python
import functools
import math

import jax
import jax.numpy as jnp
from jax import lax
from jax.experimental import pallas as pl
from jax.experimental.pallas import tpu as pltpu
from jax.sharding import PartitionSpec as P

LANES = 128
MIB = 1024 * 1024
ANY = pl.BlockSpec(memory_space=pl.ANY)
VMEM = pl.BlockSpec(memory_space=pltpu.VMEM)
SMEM = pl.BlockSpec(memory_space=pltpu.SMEM)


def call(kernel, outs, operands, specs, scratch=(), mib=12, flops=0, out_specs=None):
    arrays = list(operands) + (outs if isinstance(outs, list) else [outs])
    moved = sum(math.prod(v.shape) * jnp.dtype(v.dtype).itemsize for v in arrays)
    return pl.pallas_call(
        kernel,
        out_shape=outs,
        in_specs=specs,
        out_specs=out_specs or ([VMEM] * len(outs) if isinstance(outs, list) else VMEM),
        scratch_shapes=list(scratch),
        compiler_params=pltpu.CompilerParams(vmem_limit_bytes=mib * MIB),
        cost_estimate=pl.CostEstimate(flops=flops, transcendentals=0, bytes_accessed=moved),
    )(*operands)


def shape(*dims):
    return jax.ShapeDtypeStruct(dims, jnp.bfloat16)


def fetch(sources, first, width, stage, sems, start_row=0, start_sem=0):
    copies, at = [], start_row
    for i, source in enumerate(sources):
        rows = source.shape[0]
        copy = pltpu.make_async_copy(
            source.at[:, pl.ds(first, width)], stage.at[pl.ds(at, rows), :], sems.at[start_sem + i]
        )
        copy.start()
        copies.append(copy)
        at += rows
    return copies


def in_hbm(values):
    return pltpu.with_memory_space_constraint(values, pltpu.HBM)


def in_vmem(values):
    return pltpu.with_memory_space_constraint(values, pltpu.VMEM)


def send(values, axis, pairs, place=in_vmem):
    return place(lax.ppermute(values, axis, pairs))


def swap(values, axis, size, offset, place=in_vmem):
    return send(values, axis, [(i, i ^ offset) for i in range(size)], place)


STRAIGHT = [(i, i ^ (4 if i % 2 else 2)) for i in range(8)]
CROSSWISE = [(i, i ^ (2 if i % 2 else 4)) for i in range(8)]


def gather_rows(block, corner_hold=(), back=((), (), ()), in_turn=False, place=in_vmem):
    sibling = swap(block, "expert", 8, 1, place)
    first = send(block, "expert", STRAIGHT, place)
    second = send(sibling, "expert", STRAIGHT, place)
    hold = (*corner_hold, second) if in_turn else corner_hold
    corner = send(after((first,), *hold)[0], "expert", CROSSWISE, place)
    places = (in_vmem, in_vmem, in_vmem)
    over = [
        swap(after((v,), *holds)[0], "expert", 8, 1, last)
        for v, holds, last in zip((first, second, corner), back, places)
    ]
    return [block, sibling, first, second, corner] + over


def block_offsets(me):
    straight = jnp.where(me % 2 == 0, 2, 4).astype(jnp.int32)
    crosswise = 6 - straight
    return [0, 1, straight, straight + 1, 6, crosswise + 1, crosswise, 7]


def after(values, *others):
    return lax.optimization_barrier((*values, *others))[: len(values)] if others else values


def lead_kernel(units, width, plan_ref, *refs):
    pre_hbm, probs_hbm, names_hbm, grad_ref, own_ref, near_ref, rest_ref, keep_ref = refs[:8]
    pre_ref, probs_ref, names_ref, sems = refs[8:]
    tokens = own_ref.shape[0]
    used = 2 * units + LANES
    inputs = []
    for i, pair in enumerate(((names_hbm, names_ref), (probs_hbm, probs_ref), (pre_hbm, pre_ref))):
        inputs.append(pltpu.make_async_copy(*pair, sems.at[6 + i]))
        inputs[-1].start()
    targets = [
        own_ref.at[:, pl.ds(used, width)],
        near_ref.at[:, pl.ds(used, width)],
        keep_ref.at[:, pl.ds(0, width)],
    ] + [rest_ref.at[:, pl.ds(i * width, width)] for i in range(3)]
    copies = []
    for i, target in enumerate(targets):
        at = pl.multiple_of(plan_ref[i] * width, LANES)
        copies.append(pltpu.make_async_copy(grad_ref.at[:, pl.ds(at, width)], target, sems.at[i]))
        copies[-1].start()
    for copy in inputs:
        copy.wait()
    probs = probs_ref[...].astype(jnp.float32).T
    names = names_ref[...].astype(jnp.float32).T
    for k in range(2):
        gate = pre_ref[:, k, :units].astype(jnp.float32)
        up = pre_ref[:, k, units:].astype(jnp.float32)
        hidden = (gate * jax.nn.sigmoid(gate) * up).astype(jnp.bfloat16).astype(jnp.float32)
        scaled = (hidden * probs[:, k : k + 1]).astype(jnp.bfloat16)
        own_ref[:, k * units : (k + 1) * units] = scaled
        near_ref[:, k * units : (k + 1) * units] = scaled
    lane = lax.broadcasted_iota(jnp.int32, (tokens, LANES), 1)
    wide = jnp.where(lane == 0, names[:, 0:1], jnp.where(lane == 1, names[:, 1:2], 0.0)).astype(jnp.bfloat16)
    own_ref[:, 2 * units : used] = wide
    near_ref[:, 2 * units : used] = wide
    for copy in copies:
        copy.wait()


def masked(stage, out_ref, units, per_device, tokens, base):
    for d in range(stage.shape[0] // tokens):
        rows = pl.ds(d * tokens, tokens)
        names = stage[rows, 2 * units : 2 * units + LANES].astype(jnp.float32)
        values = [stage[rows, k * units : (k + 1) * units].astype(jnp.float32) for k in range(2)]
        for j in range(per_device):
            expert = (base + j).astype(jnp.float32)
            part = jnp.zeros((tokens, units), jnp.float32)
            for k in range(2):
                part = part + jnp.where(names[:, k : k + 1] == expert, values[k], 0.0)
            out_ref[j * units : (j + 1) * units, d * tokens : (d + 1) * tokens] = part.T.astype(jnp.bfloat16)


def times_weight(rows, weight):
    return lax.dot_general(rows, weight, (((1,), (1,)), ((), ())), preferred_element_type=jnp.float32)


def wait_all(copies):
    for copy in copies:
        copy.wait()


def turn_kernel(width, plan_ref, weight_hbm, out_ref, weight, sems):
    loads = []
    for q in range(3):
        at = pl.multiple_of(plan_ref[q + 1] * width, LANES)
        loads.append(pltpu.make_async_copy(weight_hbm.at[:, pl.ds(at, width)], weight.at[q], sems.at[q]))
        loads[-1].start()
    for q in range(3):
        loads[q].wait()
        out_ref[q * width : (q + 1) * width, :] = weight[q].T


def early_kernel(units, per_device, tokens, count, width, capacity, plan_ref, weight_hbm, *refs):
    sources = refs[:count]
    total_ref, chosen_ref, stage, weight, picked, sems = refs[count:]
    at = pl.multiple_of(plan_ref[0] * width, LANES)
    loaded = pltpu.make_async_copy(weight_hbm.at[:, pl.ds(at, width)], weight, sems.at[count])
    loaded.start()
    wait_all(fetch(sources, 2 * units, LANES + width, stage, sems))
    lane = lax.broadcasted_iota(jnp.int32, (tokens, LANES), 1)
    row = lax.broadcasted_iota(jnp.int32, (tokens, tokens), 0)
    col = lax.broadcasted_iota(jnp.int32, (tokens, tokens), 1)
    earlier = (row > col).astype(jnp.bfloat16)
    expert = (plan_ref[4] + lane // capacity).astype(jnp.float32)
    place = (lane % capacity).astype(jnp.float32)
    span = per_device * capacity
    usable = lane < span
    blocks = stage.shape[0] // tokens
    for d in range(blocks):
        rows = pl.ds(d * tokens, tokens)
        names = stage[rows, :LANES].astype(jnp.float32)
        named = ((names[:, 0:1] == expert) | (names[:, 1:2] == expert)) & usable
        rank = jnp.dot(earlier, named.astype(jnp.bfloat16), preferred_element_type=jnp.float32)
        chosen = jnp.where(named & (rank == place), 1.0, 0.0).T.astype(jnp.bfloat16)
        chosen_ref[d * span : (d + 1) * span, :] = chosen[:span, :]
        pick(chosen[:span, :], stage[rows, LANES:], picked, d, blocks, capacity)
    loaded.wait()
    for j in range(per_device):
        rows = pl.ds(j * blocks * capacity, blocks * capacity)
        total_ref[rows, :] = times_weight(picked[rows, :].astype(jnp.bfloat16), weight[j * units : (j + 1) * units, :])


def pick(chosen, values, picked, d, blocks, capacity):
    rows = jnp.dot(chosen, values, preferred_element_type=jnp.float32)
    for j in range(chosen.shape[0] // capacity):
        picked[pl.ds((j * blocks + d) * capacity, capacity), :] = rows[j * capacity : (j + 1) * capacity, :]


def first_kernel(units, per_device, tokens, count, width, started, plan_ref, *refs):
    sources = refs[started : started + count]
    hidden_hbm, *out_refs, hidden_ref, stage, sems = refs[started + count :]
    used = 2 * units + LANES
    wait_all(fetch(sources, 0, used + width, stage, sems))
    masked(stage, hidden_ref, units, per_device, tokens, plan_ref[4])
    stored = pltpu.make_async_copy(hidden_ref, hidden_hbm, sems.at[count])
    stored.start()
    part = jnp.dot(hidden_ref[...], stage[:, used:], preferred_element_type=jnp.float32)
    part = part + refs[0][...] if started else part
    at = 0
    for out_ref in out_refs:
        out_ref[...] = part[at : at + out_ref.shape[0], :].astype(out_ref.dtype)
        at += out_ref.shape[0]
    stored.wait()


def project_kernel(units, per_device, tokens, count, width, capacity, plan_ref, *refs):
    total_ref, chosen_ref, weight = refs[:3]
    sources = refs[3 : 3 + count]
    packed_ref, stage, picked, sems = refs[3 + count :]
    wait_all(fetch(sources, 0, 3 * width, stage, sems))
    span = per_device * capacity
    blocks = stage.shape[0] // tokens
    for d in range(blocks):
        pick(
            chosen_ref[d * span : (d + 1) * span, :],
            stage[pl.ds(d * tokens, tokens), :],
            picked,
            d,
            blocks,
            capacity,
        )
    projected = []
    for j in range(per_device):
        rows = pl.ds(j * blocks * capacity, blocks * capacity)
        part = jnp.dot(
            picked[rows, :].astype(jnp.bfloat16),
            weight[:, j * units : (j + 1) * units],
            preferred_element_type=jnp.float32,
        )
        projected.append(total_ref[rows, :] + part)
    for d in range(blocks):
        to = pl.multiple_of(plan_ref[5 + d] * span, 8)
        block = jnp.concatenate([values[d * capacity : (d + 1) * capacity, :] for values in projected], 0)
        packed_ref[pl.ds(to, span), :] = block.astype(jnp.bfloat16)


def columns_kernel(parts, width, *refs):
    at = len(parts)
    out_ref, hidden_ref, stage, sems = refs[-4:]
    waits, row, sem = [], 0, 0
    for i, (count, first) in enumerate(parts):
        sources = refs[at : at + count]
        rows = sum(source.shape[0] for source in sources)
        copies = fetch(sources, first, width, stage, sems, row, sem)
        copies.append(
            pltpu.make_async_copy(refs[i], hidden_ref.at[:, pl.ds(row, rows)], sems.at[sem + count])
        )
        copies[-1].start()
        waits.append((pl.ds(row, rows), copies))
        row += rows
        sem += count + 1
        at += count
    for i, (rows, copies) in enumerate(waits):
        wait_all(copies)
        part = jnp.dot(hidden_ref[:, rows], stage[rows, :], preferred_element_type=jnp.float32)
        out_ref[...] = part if i == 0 else out_ref[...] + part


def ready_kernel(units, capacity, names_ref, pre_ref, probs_ref, chosen_ref, hidden_ref, factor_ref, wide_ref):
    tokens = names_ref.shape[1]
    slots = chosen_ref.shape[2]
    experts = slots // capacity
    e_lane = lax.broadcasted_iota(jnp.int32, (tokens, experts), 1).astype(jnp.float32)
    row = lax.broadcasted_iota(jnp.int32, (tokens, tokens), 0)
    col = lax.broadcasted_iota(jnp.int32, (tokens, tokens), 1)
    earlier = (row > col).astype(jnp.bfloat16)
    names = names_ref[...].astype(jnp.float32).T
    hits = [names[:, k : k + 1] == e_lane for k in range(2)]
    rank = jnp.dot(earlier, (hits[0] | hits[1]).astype(jnp.bfloat16), preferred_element_type=jnp.float32)
    lane = lax.broadcasted_iota(jnp.int32, (tokens, slots), 1).astype(jnp.float32)
    probs = probs_ref[...].astype(jnp.float32).T
    for k in range(2):
        mine = jnp.sum(jnp.where(hits[k], rank, 0.0), axis=1, keepdims=True)
        chosen_ref[k] = (lane == names[:, k : k + 1] * capacity + mine).astype(jnp.bfloat16)
        gate = pre_ref[:, k, :units].astype(jnp.float32)
        up = pre_ref[:, k, units:].astype(jnp.float32)
        sigmoid = jax.nn.sigmoid(gate)
        silu = gate * sigmoid
        hidden_ref[k] = (silu * up).astype(jnp.bfloat16)
        factor_ref[k, :, :units] = up * sigmoid * (1.0 + gate * (1.0 - sigmoid))
        factor_ref[k, :, units:] = silu
        wide_ref[k] = jnp.broadcast_to(probs[:, k : k + 1], wide_ref.shape[1:])


def finish_kernel(units, chosen_ref, hidden_ref, factor_ref, wide_ref, packed_ref, grad_ref, grad_probs_ref):
    tokens = grad_ref.shape[0]
    sums = []
    for k in range(2):
        projected = jnp.dot(chosen_ref[k], packed_ref[...], preferred_element_type=jnp.float32)
        sums.append(jnp.sum(projected * hidden_ref[k].astype(jnp.float32), axis=1, keepdims=True))
        wide = (wide_ref[k][:, :1] * projected).astype(jnp.bfloat16).astype(jnp.float32)
        grad_ref[:, k, :units] = (wide * factor_ref[k, :, :units]).astype(jnp.bfloat16)
        grad_ref[:, k, units:] = (wide * factor_ref[k, :, units:]).astype(jnp.bfloat16)
    pair = lax.broadcasted_iota(jnp.int32, (tokens, LANES), 1)
    both = jnp.where(pair == 0, sums[0], jnp.where(pair == 1, sums[1], 0.0))
    grad_probs_ref[...] = both.T[:2, :].astype(jnp.bfloat16)


def add_kernel(count, kept_ref, *refs):
    out_ref, stage, sems = refs[count:]
    copies, at = [], 0
    for i, ref in enumerate(refs[:count]):
        rows = pl.ds(at, ref.shape[0])
        copies.append((rows, pltpu.make_async_copy(ref, stage.at[rows, :], sems.at[i])))
        copies[-1][1].start()
        at += ref.shape[0]
    for rows, copy in copies:
        copy.wait()
        out_ref[rows, :] = (kept_ref[rows, :] + stage[rows, :].astype(jnp.float32)).astype(jnp.bfloat16)


def local(grad_out, saved_pre, gate_probs, routes, down_weight):
    devices = lax.axis_size("expert")
    planes = lax.axis_size("dp")
    per_device, units, model_width = down_weight.shape
    tokens, per_token = routes.shape
    experts = per_device * devices
    capacity = 2 * tokens * per_token // experts
    me = lax.axis_index("expert").astype(jnp.int32)
    plane = lax.axis_index("dp").astype(jnp.int32)
    paired = planes == 4 and devices == 8
    width = model_width // 4
    used = per_token * units + LANES
    held = per_device * units
    everyone = devices * tokens

    if paired:
        near = plane ^ 1
        give, keep = 3 - plane, plane
        order = [give, 3 - near, keep, keep, 3 - near, near]
        order[1] = 3 - near
        sends = [give, 3 - near, near, keep, 3 - near, near]
    else:
        sends = [jnp.int32(i) for i in (0, 0, 0, 1, 2, 3)]
    plan = jnp.stack(sends).astype(jnp.int32)

    def staged(rows, columns):
        return pltpu.VMEM((rows, columns), jnp.bfloat16)

    lead, near_lead, rest, near_keep = call(
        functools.partial(lead_kernel, units, width),
        [
            shape(tokens, used + width),
            shape(tokens, used + width),
            shape(tokens, 3 * width),
            shape(tokens, width),
        ],
        [plan] + [in_hbm(v) for v in (saved_pre, gate_probs.T, routes.T, grad_out)],
        [SMEM] + [ANY] * 4,
        [
            pltpu.VMEM(saved_pre.shape, jnp.bfloat16),
            pltpu.VMEM((per_token, tokens), jnp.bfloat16),
            pltpu.VMEM((per_token, tokens), jnp.int32),
            pltpu.SemaphoreType.DMA((9,)),
        ],
    )

    def first(sources, plan, initial=(), cuts=(held,)):
        rows = sum(source.shape[0] for source in sources)
        kind = jnp.float32 if len(cuts) == 1 else jnp.bfloat16
        return call(
            functools.partial(first_kernel, units, per_device, tokens, len(sources), width, len(initial)),
            [shape(held, rows)] + [jax.ShapeDtypeStruct((cut, width), kind) for cut in cuts],
            [plan, *initial] + sources,
            [SMEM] + [VMEM] * len(initial) + [ANY] * len(sources),
            [staged(held, rows), staged(rows, used + width), pltpu.SemaphoreType.DMA((len(sources) + 1,))],
            mib=16,
            flops=2 * rows * held * width,
            out_specs=[pl.BlockSpec(memory_space=pltpu.HBM)] + [VMEM] * len(cuts),
        )

    def early(sources, plan, weight):
        rows = sum(source.shape[0] for source in sources)
        return call(
            functools.partial(early_kernel, units, per_device, tokens, len(sources), width, capacity),
            [
                jax.ShapeDtypeStruct((rows // tokens * per_device * capacity, units), jnp.float32),
                shape(rows // tokens * per_device * capacity, LANES),
            ],
            [plan, weight] + sources,
            [SMEM] + [ANY] * (1 + len(sources)),
            [
                staged(rows, LANES + width),
                staged(held, width),
                pltpu.VMEM((rows // tokens * per_device * capacity, width), jnp.float32),
                pltpu.SemaphoreType.DMA((len(sources) + 1,)),
            ],
            mib=16,
            flops=2 * rows * held * width,
        )

    def turn(plan, weight):
        return call(
            functools.partial(turn_kernel, width),
            shape(3 * width, held),
            [plan, weight],
            [SMEM, ANY],
            [pltpu.VMEM((3, held, width), jnp.bfloat16), pltpu.SemaphoreType.DMA((3,))],
        )

    def project(total, chosen, turned, sources, plan):
        rows = sum(source.shape[0] for source in sources)
        return call(
            functools.partial(project_kernel, units, per_device, tokens, len(sources), width, capacity),
            shape(rows // tokens * per_device * capacity, units),
            [plan, total, chosen, turned] + sources,
            [SMEM] + [VMEM] * 3 + [ANY] * len(sources),
            [
                staged(rows, 3 * width),
                pltpu.VMEM((rows // tokens * per_device * capacity, 3 * width), jnp.float32),
                pltpu.SemaphoreType.DMA((len(sources),)),
            ],
            mib=24,
            flops=6 * rows * held * width,
        )

    def columns(hiddens, groups):
        sources = sum([list(group) for group, _ in groups], [])
        rows = sum(source.shape[0] for source in sources)
        return call(
            functools.partial(columns_kernel, [(len(group), at) for group, at in groups], width),
            jax.ShapeDtypeStruct((held, width), jnp.float32),
            hiddens + sources,
            [ANY] * (len(hiddens) + len(sources)),
            [
                staged(held, rows),
                staged(rows, width),
                pltpu.SemaphoreType.DMA((len(hiddens) + len(sources),)),
            ],
            mib=16,
            flops=2 * rows * held * width,
        )

    weight = in_hbm(down_weight.reshape(held, model_width))
    base = me * per_device
    if paired:
        plan = jnp.stack(
            [give, keep, 3 - near, near, base] + [me ^ offset for offset in block_offsets(me)]
        ).astype(jnp.int32)
        block = swap(near_lead, "dp", 4, 1)
        own = gather_rows(lead, (), ((block,), (), ()))
        hidden, given = first(own, plan)
        hidden = in_hbm(hidden)
        near_rows = gather_rows(after((block,), own[2], own[3])[0], (), ((given,), (given,), (given,)))
        near_hidden, *given = first(near_rows, plan, [given], (held // 8, 5 * held // 16, 9 * held // 16))
        crossed = [lax.ppermute(part, "dp", [(0, 3), (3, 0), (1, 2), (2, 1)]) for part in given]
        near_hidden = in_hbm(near_hidden)
        near_keep = lax.ppermute(after((near_keep,), own[4])[0], "dp", [(i, i ^ 1) for i in range(4)])
        rest = after((jnp.concatenate([rest, near_keep], 1),), near_rows[6], near_rows[7])[0]
        total, chosen = early([in_hbm(v) for v in own], plan, after((weight,), crossed[0])[0])
        turned = turn(plan, after((weight,), given[0])[0])
        rests = gather_rows(in_hbm(rest), (crossed[0], turned), ((), (), (crossed[1], total)), True, in_hbm)
        packed = in_vmem(project(total, chosen, turned, rests, plan))
        late = [in_hbm(v) for v in after(tuple(rests[5:]), packed)]
        kept = columns([hidden, near_hidden], [(rests[:5] + late, 0), (rests[:5] + late, 3 * width)])
    else:
        own = lax.all_gather(lead, "expert", axis=0, tiled=True)
        rests = lax.all_gather(rest, "expert", axis=0, tiled=True)
        group = math.gcd(devices, 8)
        plan = jnp.concatenate(
            [jnp.arange(4, dtype=jnp.int32), base.reshape(1), jnp.arange(group, dtype=jnp.int32)]
        )
        partial, packs = 0.0, []
        for i in range(0, devices, group):
            rows = slice(i * tokens, (i + group) * tokens)
            hidden, given = first([own[rows]], plan)
            total, chosen = early([own[rows]], plan, weight)
            packs.append(project(total, chosen, turn(plan, weight), [rests[rows]], plan))
            kept = [columns([hidden], [([rests[rows]], q * width)]) for q in range(3)]
            partial = partial + jnp.concatenate([given] + kept, 1)
        packed = jnp.concatenate(packs, 0)
        summed = lax.psum_scatter(partial.astype(jnp.bfloat16), "dp", scatter_dimension=1, tiled=True)

    returned = in_vmem(lax.all_to_all(packed, "expert", 0, 0, tiled=True))
    slots = devices * per_device * capacity
    ready = call(
        functools.partial(ready_kernel, units, capacity),
        [
            shape(per_token, tokens, slots),
            shape(per_token, tokens, units),
            jax.ShapeDtypeStruct((per_token, tokens, 2 * units), jnp.float32),
            jax.ShapeDtypeStruct((per_token, tokens, LANES), jnp.float32),
        ],
        [after((routes.T,), kept if paired else packed)[0], saved_pre, gate_probs.T],
        [VMEM] * 3,
    )
    grad_pre, grad_probs = call(
        functools.partial(finish_kernel, units),
        [shape(tokens, per_token, 2 * units), shape(per_token, tokens)],
        [in_vmem(values) for values in ready] + [returned],
        [VMEM] * 5,
    )
    if paired:
        settled = [in_hbm(crossed[0]), in_hbm(after((crossed[1],), packed)[0])]
        crossed = settled + list(after(crossed[-1:], grad_probs))
        summed = call(
            functools.partial(add_kernel, len(crossed)),
            shape(held, width),
            [kept] + crossed,
            [VMEM] + [ANY] * len(crossed),
            [staged(held, width), pltpu.SemaphoreType.DMA((len(crossed),))],
        )
    return grad_pre, grad_probs.T, summed.reshape(per_device, units, model_width // planes)


def solution(mesh):
    in_specs = (
        P(("dp", "expert"), None),
        P(("dp", "expert"), None, None),
        P(("dp", "expert"), None),
        P(("dp", "expert"), None),
        P("expert", None, None),
    )
    out_specs = (
        P(("dp", "expert"), None, None),
        P(("dp", "expert"), None),
        P("expert", None, "dp"),
    )
    return jax.shard_map(local, mesh=mesh, in_specs=in_specs, out_specs=out_specs, check_vma=False)
```

```python
import functools
import math

import jax
import jax.numpy as jnp
from jax import lax
from jax.experimental import pallas as pl
from jax.experimental.pallas import tpu as pltpu
from jax.sharding import PartitionSpec as P

LANES = 128
MIB = 1024 * 1024
ANY = pl.BlockSpec(memory_space=pl.ANY)
VMEM = pl.BlockSpec(memory_space=pltpu.VMEM)
SMEM = pl.BlockSpec(memory_space=pltpu.SMEM)


def call(kernel, outs, operands, specs, scratch=(), mib=12, flops=0, out_specs=None):
    arrays = list(operands) + (outs if isinstance(outs, list) else [outs])
    moved = sum(math.prod(v.shape) * jnp.dtype(v.dtype).itemsize for v in arrays)
    return pl.pallas_call(
        kernel,
        out_shape=outs,
        in_specs=specs,
        out_specs=out_specs or ([VMEM] * len(outs) if isinstance(outs, list) else VMEM),
        scratch_shapes=list(scratch),
        compiler_params=pltpu.CompilerParams(vmem_limit_bytes=mib * MIB),
        cost_estimate=pl.CostEstimate(flops=flops, transcendentals=0, bytes_accessed=moved),
    )(*operands)


def shape(*dims):
    return jax.ShapeDtypeStruct(dims, jnp.bfloat16)


def fetch(sources, first, width, stage, sems, start_row=0, start_sem=0):
    copies, at = [], start_row
    for i, source in enumerate(sources):
        rows = source.shape[0]
        copy = pltpu.make_async_copy(
            source.at[:, pl.ds(first, width)], stage.at[pl.ds(at, rows), :], sems.at[start_sem + i]
        )
        copy.start()
        copies.append(copy)
        at += rows
    return copies


def in_hbm(values):
    return pltpu.with_memory_space_constraint(values, pltpu.HBM)


def in_vmem(values):
    return pltpu.with_memory_space_constraint(values, pltpu.VMEM)


def send(values, axis, pairs, place=in_vmem):
    return place(lax.ppermute(values, axis, pairs))


def swap(values, axis, size, offset, place=in_vmem):
    return send(values, axis, [(i, i ^ offset) for i in range(size)], place)


STRAIGHT = [(i, i ^ (4 if i % 2 else 2)) for i in range(8)]
CROSSWISE = [(i, i ^ (2 if i % 2 else 4)) for i in range(8)]


def gather_rows(block, corner_hold=(), back=((), (), ()), in_turn=False, place=in_vmem):
    sibling = swap(block, "expert", 8, 1, place)
    first = send(block, "expert", STRAIGHT, place)
    second = send(sibling, "expert", STRAIGHT, place)
    hold = (*corner_hold, second) if in_turn else corner_hold
    corner = send(after((first,), *hold)[0], "expert", CROSSWISE, place)
    places = (in_vmem, in_vmem, in_vmem)
    over = [
        swap(after((v,), *holds)[0], "expert", 8, 1, last)
        for v, holds, last in zip((first, second, corner), back, places)
    ]
    return [block, sibling, first, second, corner] + over


def block_offsets(me):
    straight = jnp.where(me % 2 == 0, 2, 4).astype(jnp.int32)
    crosswise = 6 - straight
    return [0, 1, straight, straight + 1, 6, crosswise + 1, crosswise, 7]


def after(values, *others):
    return lax.optimization_barrier((*values, *others))[: len(values)] if others else values


def lead_kernel(units, width, plan_ref, *refs):
    pre_hbm, probs_hbm, names_hbm, grad_ref, own_ref, near_ref, rest_ref, keep_ref = refs[:8]
    pre_ref, probs_ref, names_ref, sems = refs[8:]
    tokens = own_ref.shape[0]
    used = 2 * units + LANES
    inputs = []
    for i, pair in enumerate(((names_hbm, names_ref), (probs_hbm, probs_ref), (pre_hbm, pre_ref))):
        inputs.append(pltpu.make_async_copy(*pair, sems.at[6 + i]))
        inputs[-1].start()
    targets = [
        own_ref.at[:, pl.ds(used, width)],
        near_ref.at[:, pl.ds(used, width)],
        keep_ref.at[:, pl.ds(0, width)],
    ] + [rest_ref.at[:, pl.ds(i * width, width)] for i in range(3)]
    copies = []
    for i, target in enumerate(targets):
        at = pl.multiple_of(plan_ref[i] * width, LANES)
        copies.append(pltpu.make_async_copy(grad_ref.at[:, pl.ds(at, width)], target, sems.at[i]))
        copies[-1].start()
    for copy in inputs:
        copy.wait()
    probs = probs_ref[...].astype(jnp.float32).T
    names = names_ref[...].astype(jnp.float32).T
    for k in range(2):
        gate = pre_ref[:, k, :units].astype(jnp.float32)
        up = pre_ref[:, k, units:].astype(jnp.float32)
        hidden = (gate * jax.nn.sigmoid(gate) * up).astype(jnp.bfloat16).astype(jnp.float32)
        scaled = (hidden * probs[:, k : k + 1]).astype(jnp.bfloat16)
        own_ref[:, k * units : (k + 1) * units] = scaled
        near_ref[:, k * units : (k + 1) * units] = scaled
    lane = lax.broadcasted_iota(jnp.int32, (tokens, LANES), 1)
    wide = jnp.where(lane == 0, names[:, 0:1], jnp.where(lane == 1, names[:, 1:2], 0.0)).astype(jnp.bfloat16)
    own_ref[:, 2 * units : used] = wide
    near_ref[:, 2 * units : used] = wide
    for copy in copies:
        copy.wait()


def masked(stage, out_ref, units, per_device, tokens, base):
    for d in range(stage.shape[0] // tokens):
        rows = pl.ds(d * tokens, tokens)
        names = stage[rows, 2 * units : 2 * units + LANES].astype(jnp.float32)
        values = [stage[rows, k * units : (k + 1) * units].astype(jnp.float32) for k in range(2)]
        for j in range(per_device):
            expert = (base + j).astype(jnp.float32)
            part = jnp.zeros((tokens, units), jnp.float32)
            for k in range(2):
                part = part + jnp.where(names[:, k : k + 1] == expert, values[k], 0.0)
            out_ref[j * units : (j + 1) * units, d * tokens : (d + 1) * tokens] = part.T.astype(jnp.bfloat16)


def times_weight(rows, weight):
    return lax.dot_general(rows, weight, (((1,), (1,)), ((), ())), preferred_element_type=jnp.float32)


def wait_all(copies):
    for copy in copies:
        copy.wait()


def turn_kernel(width, plan_ref, weight_hbm, out_ref, weight, sems):
    loads = []
    for q in range(3):
        at = pl.multiple_of(plan_ref[q + 1] * width, LANES)
        loads.append(pltpu.make_async_copy(weight_hbm.at[:, pl.ds(at, width)], weight.at[q], sems.at[q]))
        loads[-1].start()
    for q in range(3):
        loads[q].wait()
        out_ref[q * width : (q + 1) * width, :] = weight[q].T


def early_kernel(units, per_device, tokens, count, width, capacity, plan_ref, weight_hbm, *refs):
    sources = refs[:count]
    total_ref, chosen_ref, stage, weight, picked, sems = refs[count:]
    at = pl.multiple_of(plan_ref[0] * width, LANES)
    loaded = pltpu.make_async_copy(weight_hbm.at[:, pl.ds(at, width)], weight, sems.at[count])
    loaded.start()
    wait_all(fetch(sources, 2 * units, LANES + width, stage, sems))
    lane = lax.broadcasted_iota(jnp.int32, (tokens, LANES), 1)
    row = lax.broadcasted_iota(jnp.int32, (tokens, tokens), 0)
    col = lax.broadcasted_iota(jnp.int32, (tokens, tokens), 1)
    earlier = (row > col).astype(jnp.bfloat16)
    expert = (plan_ref[4] + lane // capacity).astype(jnp.float32)
    place = (lane % capacity).astype(jnp.float32)
    span = per_device * capacity
    usable = lane < span
    blocks = stage.shape[0] // tokens
    for d in range(blocks):
        rows = pl.ds(d * tokens, tokens)
        names = stage[rows, :LANES].astype(jnp.float32)
        named = ((names[:, 0:1] == expert) | (names[:, 1:2] == expert)) & usable
        rank = jnp.dot(earlier, named.astype(jnp.bfloat16), preferred_element_type=jnp.float32)
        chosen = jnp.where(named & (rank == place), 1.0, 0.0).T.astype(jnp.bfloat16)
        chosen_ref[d * span : (d + 1) * span, :] = chosen[:span, :]
        pick(chosen[:span, :], stage[rows, LANES:], picked, d, blocks, capacity)
    loaded.wait()
    for j in range(per_device):
        rows = pl.ds(j * blocks * capacity, blocks * capacity)
        total_ref[rows, :] = times_weight(picked[rows, :].astype(jnp.bfloat16), weight[j * units : (j + 1) * units, :])


def pick(chosen, values, picked, d, blocks, capacity):
    rows = jnp.dot(chosen, values, preferred_element_type=jnp.float32)
    for j in range(chosen.shape[0] // capacity):
        picked[pl.ds((j * blocks + d) * capacity, capacity), :] = rows[j * capacity : (j + 1) * capacity, :]


def first_kernel(units, per_device, tokens, count, width, started, plan_ref, *refs):
    sources = refs[started : started + count]
    hidden_hbm, *out_refs, hidden_ref, stage, sems = refs[started + count :]
    used = 2 * units + LANES
    wait_all(fetch(sources, 0, used + width, stage, sems))
    masked(stage, hidden_ref, units, per_device, tokens, plan_ref[4])
    stored = pltpu.make_async_copy(hidden_ref, hidden_hbm, sems.at[count])
    stored.start()
    part = jnp.dot(hidden_ref[...], stage[:, used:], preferred_element_type=jnp.float32)
    part = part + refs[0][...] if started else part
    at = 0
    for out_ref in out_refs:
        out_ref[...] = part[at : at + out_ref.shape[0], :].astype(out_ref.dtype)
        at += out_ref.shape[0]
    stored.wait()


def project_kernel(units, per_device, tokens, count, width, capacity, plan_ref, *refs):
    total_ref, chosen_ref, weight = refs[:3]
    sources = refs[3 : 3 + count]
    packed_ref, stage, picked, sems = refs[3 + count :]
    wait_all(fetch(sources, 0, 3 * width, stage, sems))
    span = per_device * capacity
    blocks = stage.shape[0] // tokens
    for d in range(blocks):
        pick(
            chosen_ref[d * span : (d + 1) * span, :],
            stage[pl.ds(d * tokens, tokens), :],
            picked,
            d,
            blocks,
            capacity,
        )
    projected = []
    for j in range(per_device):
        rows = pl.ds(j * blocks * capacity, blocks * capacity)
        part = jnp.dot(
            picked[rows, :].astype(jnp.bfloat16),
            weight[:, j * units : (j + 1) * units],
            preferred_element_type=jnp.float32,
        )
        projected.append(total_ref[rows, :] + part)
    for d in range(blocks):
        to = pl.multiple_of(plan_ref[5 + d] * span, 8)
        block = jnp.concatenate([values[d * capacity : (d + 1) * capacity, :] for values in projected], 0)
        packed_ref[pl.ds(to, span), :] = block.astype(jnp.bfloat16)


def columns_kernel(parts, width, *refs):
    at = len(parts)
    out_ref, hidden_ref, stage, sems = refs[-4:]
    waits, row, sem = [], 0, 0
    for i, (count, first) in enumerate(parts):
        sources = refs[at : at + count]
        rows = sum(source.shape[0] for source in sources)
        copies = fetch(sources, first, width, stage, sems, row, sem)
        copies.append(
            pltpu.make_async_copy(refs[i], hidden_ref.at[:, pl.ds(row, rows)], sems.at[sem + count])
        )
        copies[-1].start()
        waits.append((pl.ds(row, rows), copies))
        row += rows
        sem += count + 1
        at += count
    for i, (rows, copies) in enumerate(waits):
        wait_all(copies)
        part = jnp.dot(hidden_ref[:, rows], stage[rows, :], preferred_element_type=jnp.float32)
        out_ref[...] = part if i == 0 else out_ref[...] + part


def ready_kernel(units, capacity, names_ref, pre_ref, probs_ref, chosen_ref, hidden_ref, factor_ref, wide_ref):
    tokens = names_ref.shape[1]
    slots = chosen_ref.shape[2]
    experts = slots // capacity
    e_lane = lax.broadcasted_iota(jnp.int32, (tokens, experts), 1).astype(jnp.float32)
    row = lax.broadcasted_iota(jnp.int32, (tokens, tokens), 0)
    col = lax.broadcasted_iota(jnp.int32, (tokens, tokens), 1)
    earlier = (row > col).astype(jnp.bfloat16)
    names = names_ref[...].astype(jnp.float32).T
    hits = [names[:, k : k + 1] == e_lane for k in range(2)]
    rank = jnp.dot(earlier, (hits[0] | hits[1]).astype(jnp.bfloat16), preferred_element_type=jnp.float32)
    lane = lax.broadcasted_iota(jnp.int32, (tokens, slots), 1).astype(jnp.float32)
    probs = probs_ref[...].astype(jnp.float32).T
    for k in range(2):
        mine = jnp.sum(jnp.where(hits[k], rank, 0.0), axis=1, keepdims=True)
        chosen_ref[k] = (lane == names[:, k : k + 1] * capacity + mine).astype(jnp.bfloat16)
        gate = pre_ref[:, k, :units].astype(jnp.float32)
        up = pre_ref[:, k, units:].astype(jnp.float32)
        sigmoid = jax.nn.sigmoid(gate)
        silu = gate * sigmoid
        hidden_ref[k] = (silu * up).astype(jnp.bfloat16)
        factor_ref[k, :, :units] = up * sigmoid * (1.0 + gate * (1.0 - sigmoid))
        factor_ref[k, :, units:] = silu
        wide_ref[k] = jnp.broadcast_to(probs[:, k : k + 1], wide_ref.shape[1:])


def finish_kernel(units, chosen_ref, hidden_ref, factor_ref, wide_ref, packed_ref, grad_ref, grad_probs_ref):
    tokens = grad_ref.shape[0]
    sums = []
    for k in range(2):
        projected = jnp.dot(chosen_ref[k], packed_ref[...], preferred_element_type=jnp.float32)
        sums.append(jnp.sum(projected * hidden_ref[k].astype(jnp.float32), axis=1, keepdims=True))
        wide = (wide_ref[k][:, :1] * projected).astype(jnp.bfloat16).astype(jnp.float32)
        grad_ref[:, k, :units] = (wide * factor_ref[k, :, :units]).astype(jnp.bfloat16)
        grad_ref[:, k, units:] = (wide * factor_ref[k, :, units:]).astype(jnp.bfloat16)
    pair = lax.broadcasted_iota(jnp.int32, (tokens, LANES), 1)
    both = jnp.where(pair == 0, sums[0], jnp.where(pair == 1, sums[1], 0.0))
    grad_probs_ref[...] = both.T[:2, :].astype(jnp.bfloat16)


def add_kernel(count, kept_ref, *refs):
    out_ref, stage, sems = refs[count:]
    copies, at = [], 0
    for i, ref in enumerate(refs[:count]):
        rows = pl.ds(at, ref.shape[0])
        copies.append((rows, pltpu.make_async_copy(ref, stage.at[rows, :], sems.at[i])))
        copies[-1][1].start()
        at += ref.shape[0]
    for rows, copy in copies:
        copy.wait()
        out_ref[rows, :] = (kept_ref[rows, :] + stage[rows, :].astype(jnp.float32)).astype(jnp.bfloat16)


def local(grad_out, saved_pre, gate_probs, routes, down_weight):
    devices = lax.axis_size("expert")
    planes = lax.axis_size("dp")
    per_device, units, model_width = down_weight.shape
    tokens, per_token = routes.shape
    experts = per_device * devices
    capacity = 2 * tokens * per_token // experts
    me = lax.axis_index("expert").astype(jnp.int32)
    plane = lax.axis_index("dp").astype(jnp.int32)
    paired = planes == 4 and devices == 8
    width = model_width // 4
    used = per_token * units + LANES
    held = per_device * units
    everyone = devices * tokens

    if paired:
        near = plane ^ 1
        give, keep = 3 - plane, plane
        order = [give, 3 - near, keep, keep, 3 - near, near]
        order[1] = 3 - near
        sends = [give, 3 - near, near, keep, 3 - near, near]
    else:
        sends = [jnp.int32(i) for i in (0, 0, 0, 1, 2, 3)]
    plan = jnp.stack(sends).astype(jnp.int32)

    def staged(rows, columns):
        return pltpu.VMEM((rows, columns), jnp.bfloat16)

    lead, near_lead, rest, near_keep = call(
        functools.partial(lead_kernel, units, width),
        [
            shape(tokens, used + width),
            shape(tokens, used + width),
            shape(tokens, 3 * width),
            shape(tokens, width),
        ],
        [plan] + [in_hbm(v) for v in (saved_pre, gate_probs.T, routes.T, grad_out)],
        [SMEM] + [ANY] * 4,
        [
            pltpu.VMEM(saved_pre.shape, jnp.bfloat16),
            pltpu.VMEM((per_token, tokens), jnp.bfloat16),
            pltpu.VMEM((per_token, tokens), jnp.int32),
            pltpu.SemaphoreType.DMA((9,)),
        ],
    )

    def first(sources, plan, initial=(), cuts=(held,)):
        rows = sum(source.shape[0] for source in sources)
        kind = jnp.float32 if len(cuts) == 1 else jnp.bfloat16
        return call(
            functools.partial(first_kernel, units, per_device, tokens, len(sources), width, len(initial)),
            [shape(held, rows)] + [jax.ShapeDtypeStruct((cut, width), kind) for cut in cuts],
            [plan, *initial] + sources,
            [SMEM] + [VMEM] * len(initial) + [ANY] * len(sources),
            [staged(held, rows), staged(rows, used + width), pltpu.SemaphoreType.DMA((len(sources) + 1,))],
            mib=16,
            flops=2 * rows * held * width,
            out_specs=[pl.BlockSpec(memory_space=pltpu.HBM)] + [VMEM] * len(cuts),
        )

    def early(sources, plan, weight):
        rows = sum(source.shape[0] for source in sources)
        return call(
            functools.partial(early_kernel, units, per_device, tokens, len(sources), width, capacity),
            [
                jax.ShapeDtypeStruct((rows // tokens * per_device * capacity, units), jnp.float32),
                shape(rows // tokens * per_device * capacity, LANES),
            ],
            [plan, weight] + sources,
            [SMEM] + [ANY] * (1 + len(sources)),
            [
                staged(rows, LANES + width),
                staged(held, width),
                pltpu.VMEM((rows // tokens * per_device * capacity, width), jnp.float32),
                pltpu.SemaphoreType.DMA((len(sources) + 1,)),
            ],
            mib=16,
            flops=2 * rows * held * width,
        )

    def turn(plan, weight):
        return call(
            functools.partial(turn_kernel, width),
            shape(3 * width, held),
            [plan, weight],
            [SMEM, ANY],
            [pltpu.VMEM((3, held, width), jnp.bfloat16), pltpu.SemaphoreType.DMA((3,))],
        )

    def project(total, chosen, turned, sources, plan):
        rows = sum(source.shape[0] for source in sources)
        return call(
            functools.partial(project_kernel, units, per_device, tokens, len(sources), width, capacity),
            shape(rows // tokens * per_device * capacity, units),
            [plan, total, chosen, turned] + sources,
            [SMEM] + [VMEM] * 3 + [ANY] * len(sources),
            [
                staged(rows, 3 * width),
                pltpu.VMEM((rows // tokens * per_device * capacity, 3 * width), jnp.float32),
                pltpu.SemaphoreType.DMA((len(sources),)),
            ],
            mib=24,
            flops=6 * rows * held * width,
        )

    def columns(hiddens, groups):
        sources = sum([list(group) for group, _ in groups], [])
        rows = sum(source.shape[0] for source in sources)
        return call(
            functools.partial(columns_kernel, [(len(group), at) for group, at in groups], width),
            jax.ShapeDtypeStruct((held, width), jnp.float32),
            hiddens + sources,
            [ANY] * (len(hiddens) + len(sources)),
            [
                staged(held, rows),
                staged(rows, width),
                pltpu.SemaphoreType.DMA((len(hiddens) + len(sources),)),
            ],
            mib=16,
            flops=2 * rows * held * width,
        )

    weight = in_hbm(down_weight.reshape(held, model_width))
    base = me * per_device
    if paired:
        plan = jnp.stack(
            [give, keep, 3 - near, near, base] + [me ^ offset for offset in block_offsets(me)]
        ).astype(jnp.int32)
        block = swap(near_lead, "dp", 4, 1)
        own = gather_rows(lead, (), ((block,), (), ()))
        hidden, given = first(own, plan)
        hidden = in_hbm(hidden)
        near_rows = gather_rows(after((block,), own[2], own[3])[0], (), ((given,), (given,), (given,)))
        near_hidden, *given = first(near_rows, plan, [given], (held // 16, 5 * held // 16, 5 * held // 8))
        crossed = [lax.ppermute(part, "dp", [(0, 3), (3, 0), (1, 2), (2, 1)]) for part in given]
        near_hidden = in_hbm(near_hidden)
        near_keep = lax.ppermute(after((near_keep,), own[4])[0], "dp", [(i, i ^ 1) for i in range(4)])
        rest = after((jnp.concatenate([rest, near_keep], 1),), near_rows[6], near_rows[7])[0]
        total, chosen = early([in_hbm(v) for v in own], plan, after((weight,), crossed[0])[0])
        turned = turn(plan, after((weight,), given[0])[0])
        rests = gather_rows(in_hbm(rest), (crossed[0], turned), ((), (), (crossed[1], total)), True, in_hbm)
        packed = in_vmem(project(total, chosen, turned, rests, plan))
        late = [in_hbm(v) for v in after(tuple(rests[5:]), packed)]
        kept = columns([hidden, near_hidden], [(rests[:5] + late, 0), (rests[:5] + late, 3 * width)])
    else:
        own = lax.all_gather(lead, "expert", axis=0, tiled=True)
        rests = lax.all_gather(rest, "expert", axis=0, tiled=True)
        group = math.gcd(devices, 8)
        plan = jnp.concatenate(
            [jnp.arange(4, dtype=jnp.int32), base.reshape(1), jnp.arange(group, dtype=jnp.int32)]
        )
        partial, packs = 0.0, []
        for i in range(0, devices, group):
            rows = slice(i * tokens, (i + group) * tokens)
            hidden, given = first([own[rows]], plan)
            total, chosen = early([own[rows]], plan, weight)
            packs.append(project(total, chosen, turn(plan, weight), [rests[rows]], plan))
            kept = [columns([hidden], [([rests[rows]], q * width)]) for q in range(3)]
            partial = partial + jnp.concatenate([given] + kept, 1)
        packed = jnp.concatenate(packs, 0)
        summed = lax.psum_scatter(partial.astype(jnp.bfloat16), "dp", scatter_dimension=1, tiled=True)

    returned = in_vmem(lax.all_to_all(packed, "expert", 0, 0, tiled=True))
    slots = devices * per_device * capacity
    ready = call(
        functools.partial(ready_kernel, units, capacity),
        [
            shape(per_token, tokens, slots),
            shape(per_token, tokens, units),
            jax.ShapeDtypeStruct((per_token, tokens, 2 * units), jnp.float32),
            jax.ShapeDtypeStruct((per_token, tokens, LANES), jnp.float32),
        ],
        [after((routes.T,), kept if paired else packed)[0], saved_pre, gate_probs.T],
        [VMEM] * 3,
    )
    grad_pre, grad_probs = call(
        functools.partial(finish_kernel, units),
        [shape(tokens, per_token, 2 * units), shape(per_token, tokens)],
        [in_vmem(values) for values in ready] + [returned],
        [VMEM] * 5,
    )
    if paired:
        settled = [in_hbm(crossed[0]), in_hbm(after((crossed[1],), packed)[0])]
        crossed = settled + list(after(crossed[-1:], grad_probs))
        summed = call(
            functools.partial(add_kernel, len(crossed)),
            shape(held, width),
            [kept] + crossed,
            [VMEM] + [ANY] * len(crossed),
            [staged(held, width), pltpu.SemaphoreType.DMA((len(crossed),))],
        )
    return grad_pre, grad_probs.T, summed.reshape(per_device, units, model_width // planes)


def solution(mesh):
    in_specs = (
        P(("dp", "expert"), None),
        P(("dp", "expert"), None, None),
        P(("dp", "expert"), None),
        P(("dp", "expert"), None),
        P("expert", None, None),
    )
    out_specs = (
        P(("dp", "expert"), None, None),
        P(("dp", "expert"), None),
        P("expert", None, "dp"),
    )
    return jax.shard_map(local, mesh=mesh, in_specs=in_specs, out_specs=out_specs, check_vma=False)
```
